256 devices in a mesh: tm: 32 (over y, z), mp: 8 (over x, core).
Axes of the slice: x: 4, y: 4, z: 8, core: 2. Of those that a mesh axis runs over, the one named last changes fastest.
Arguments:
- frames_in: bfloat16 [16384, 1024], P('tm'), may hold values from -16 to 16
- queries: bfloat16 [16384, 1024], P('tm', 'mp'), may hold values from -6 to 6
- keys: bfloat16 [16384, 1024], P('tm', 'mp'), may hold values from -6 to 6
- values: bfloat16 [16384, 1024], P('tm', 'mp'), may hold values from -6 to 6
- segment_edges: int32 [2, 16384], P(None, 'tm'), may hold values from 0 to 16383, as said below
- out_proj: bfloat16 [1024, 1024], P('mp'), may hold values from -0.1875 to 0.1875
- expert_ids: int32 [16384, 2], P('tm'), may hold values from 0 to 63, all different within a row; in each aligned block of 512 rows (0 to 511, 512 to 1023, ...) at most 32 rows name the same one
- gates: float32 [16384, 2], P('tm'), may hold values from 0.25 to 1
- w_gate: bfloat16 [64, 1024, 4096], P('tm', None, 'mp'), may hold values from -0.1875 to 0.1875
- w_up: bfloat16 [64, 1024, 4096], P('tm', None, 'mp'), may hold values from -0.1875 to 0.1875
- w_down: bfloat16 [64, 4096, 1024], P('tm', 'mp'), may hold values from -0.09375 to 0.09375
Outputs:
- layer_out: bfloat16 [16384, 1024], P('tm', 'mp')
The draws below stay inside these ranges and needn't reach their ends.
Inputs may be any that keep to these rules, and one draw needn't show every extreme that they name: `segment_edges`: row 0 holds the first frame of each frame's segment and row 1 its last. Segments are runs of 1 to 64 frames; every multiple of 64 starts a segment, and some segment has exactly 64 frames. `expert_ids`: each frame names 2 different experts. Among the 512 frames of one index of tm no expert is named more than 32 times; in some of these groups one expert is named exactly 32 times.
All inputs are finite; a program needn't handle non-finite values.
Results may differ from the reference program's by a relative error of at most 0.006.
Values may be sent and summed in bfloat16 or wider, within the bound.
A program may use at most 128 MiB of HBM per device.

```python
import math
import jax
import jax.numpy as jnp
import numpy as np
from jax import lax

D = 1024
HEADS = 16
HEAD = 64
FF = 4096
TOP = 2
SEGMENT = 64
LEFT = 256
F_DEV = 512
FRAMES = 16384
EXPERTS = 64
CAP = 32
N_TM = 32


def base_rows(key, salt):
    sub = jax.random.fold_in(key, salt)
    return jnp.clip(jax.random.normal(sub, (FRAMES, D), jnp.float32), -4.0, 4.0)


def draw_queries(key, part):
    rows = base_rows(key, 11)
    return rows.astype(jnp.bfloat16)


def draw_keys(key, part):
    rows = base_rows(key, 13)
    return rows.astype(jnp.bfloat16)


def draw_frames_in(key, part):
    low = jnp.log(0.2)
    high = jnp.log(2.0)
    row_scale = jnp.exp(jax.random.uniform(jax.random.fold_in(key, 1), (FRAMES, 1), jnp.float32, low, high))
    col_scale = jnp.exp(jax.random.uniform(jax.random.fold_in(key, 2), (1, D), jnp.float32, low, high))
    noise = jnp.clip(jax.random.normal(jax.random.fold_in(key, 3), (FRAMES, D), jnp.float32), -4.0, 4.0)
    return (noise * row_scale * col_scale).astype(jnp.bfloat16)


def draw_segment_edges(key, part):
    positions = jnp.arange(FRAMES, dtype=jnp.int32)
    extra = jax.random.randint(key, (FRAMES,), 0, 64) == 0
    cuts = jnp.where(positions < SEGMENT, positions == 0, (positions % SEGMENT == 0) | extra)
    first = lax.cummax(jnp.where(cuts, positions, 0), axis=0)
    starts = jnp.where(cuts, positions, FRAMES)
    following = jnp.concatenate([starts[1:], jnp.array([FRAMES], jnp.int32)])
    last = lax.cummin(following, axis=0, reverse=True) - 1
    return jnp.stack([first, last], 0).astype(jnp.int32)


def shard_levels(key, shape, shards, least, largest):
    factor_of = 1.0
    for position, parts in shards:
        heights = jax.random.uniform(jax.random.fold_in(jax.random.fold_in(key, 6), position), (parts,), jnp.float32, least / len(shards), largest / len(shards))
        factor_of = factor_of * jnp.repeat(jnp.exp(heights), shape[position] // parts).reshape((-1,) + (1,) * (len(shape) - 1 - position))
    return factor_of


def shared_out(key, own, number, rows, amount, top, bound, lean):
    sequence = jax.random.permutation(key, amount)
    packed, ordinary = shares(amount, rows * top, bound, lean, True), shares(amount, rows * top, bound, lean, False)
    places = jnp.arange(amount)

    def named(sizes, rotation):
        used = int((sizes > 0).sum())
        fixed = max(1, used // 4)
        moved = fixed + (places - fixed + rotation * (used - fixed)) % max(1, amount - fixed)
        return jnp.zeros((amount,), jnp.int32).at[sequence[jnp.where(places < fixed, places, moved)]].set(jnp.asarray(sizes, jnp.int32))

    sizes = jnp.where(number % 4 == 0, named(packed, number // 4), named(ordinary, number - number // 4 - 1))
    mixed = jax.random.permutation(jax.random.fold_in(own, 3), amount)
    giver, sink = mixed[0:amount // 2 * 2:2], mixed[1:amount // 2 * 2:2]
    margin = jnp.minimum(sizes[giver] - 1, bound - sizes[sink]) // 2
    margin = jnp.where((giver == sequence[0]) | (sink == sequence[0]) | (sizes[sink] == 0), 0, jnp.maximum(margin, 0))
    moved = jax.random.randint(jax.random.fold_in(own, 4), (amount // 2,), 0, 1 << 20) % (margin + 1)
    sizes = sizes.at[giver].add(-moved).at[sink].add(moved)
    labels = jnp.searchsorted(jnp.cumsum(sizes), jnp.arange(rows * top), side="right").astype(jnp.int32)
    listing = labels.reshape(top, rows).T
    listing = listing[jax.random.permutation(jax.random.fold_in(own, 1), rows)]
    rotation = jax.random.randint(jax.random.fold_in(own, 2), (rows, 1), 0, top)
    return jnp.take_along_axis(listing, (jnp.arange(top)[None, :] + rotation) % top, axis=1)


def shares(number_of, total, limit, skew, full):
    loads = [(1 << 20) // math.isqrt(standing ** skew) + 1 for standing in range(1, number_of + 1)]
    largest = limit if full else min(limit, max(-(-total // number_of), total * loads[0] // sum(loads)))
    least = 1 if total - largest >= number_of - 1 else 0
    given, surplus = [largest] + [least] * (number_of - 1), total - largest - least * (number_of - 1)
    while surplus > 0:
        candidates = [i for i in range(1, number_of) if given[i] < largest] or [i for i in range(1, number_of) if given[i] < limit]
        whole, remaining = sum([loads[i] for i in candidates]), surplus
        for i in candidates:
            addition = min(limit - given[i], max(1, remaining * loads[i] // whole), surplus)
            given[i] = given[i] + addition
            surplus = surplus - addition
    return np.array(given)


def gaussian(rng, shape, scale, most, shards=(), kind=jnp.bfloat16):
    values = jax.random.normal(rng, shape, jnp.float32) * scale
    if len(shards) > 0:
        values = shard_levels(rng, shape, shards, -0.22, 0.18) * values
    return jnp.clip(values, min=-most, max=most).astype(kind)


def setup_inputs(seed: int = 0) -> dict:
    key_list = jax.random.split(jax.random.key(seed), 12)
    frames_in = draw_frames_in(jax.random.fold_in(key_list[11], 71), 0)
    queries = draw_queries(jax.random.fold_in(key_list[11], 71), 0)
    keys = draw_keys(jax.random.fold_in(key_list[11], 71), 0)
    values = gaussian(key_list[3], (FRAMES, D), 1.0, 6.0, ((0, 32), (1, 8)))
    segment_edges = draw_segment_edges(jax.random.fold_in(key_list[11], 71), 0)
    out_proj = gaussian(key_list[5], (D, D), D ** -0.5, 0.1875, ((0, 8),))
    expert_ids_keys = jax.random.split(jax.random.fold_in(key_list[6], 1), FRAMES // F_DEV)
    expert_ids_turns = jax.random.permutation(jax.random.fold_in(key_list[6], 3), FRAMES // F_DEV)
    expert_ids = jax.vmap(lambda own, number: shared_out(jax.random.fold_in(key_list[6], 2), own, number, F_DEV, EXPERTS, TOP, CAP, 2))(expert_ids_keys, expert_ids_turns).reshape((FRAMES, TOP))
    gates = jnp.clip(0.25 + 0.75 * jax.random.uniform(key_list[7], (FRAMES, TOP), jnp.float32) ** shard_levels(key_list[7], (FRAMES, TOP), ((0, 32),), -0.2, 0.2), 0.25, 1.0)
    w_gate = gaussian(key_list[8], (EXPERTS, D, FF), D ** -0.5, 0.1875, ((0, 32), (2, 8)))
    w_up = gaussian(key_list[9], (EXPERTS, D, FF), D ** -0.5, 0.1875, ((0, 32), (2, 8)))
    w_down = gaussian(key_list[10], (EXPERTS, FF, D), FF ** -0.5, 0.09375, ((0, 32), (1, 8)))
    return {"frames_in": frames_in, "queries": queries, "keys": keys, "values": values, "segment_edges": segment_edges, "out_proj": out_proj, "expert_ids": expert_ids, "gates": gates, "w_gate": w_gate, "w_up": w_up, "w_down": w_down}


EPS = 1e-06

def attend(queries, keys, values, segment_edges):
    block = min(F_DEV, 512)
    head_width = HEAD
    scale = HEAD ** (-0.5)
    total = queries.shape[0]
    keys_padded = jnp.concatenate([jnp.zeros((LEFT, D), keys.dtype), keys], 0)
    values_padded = jnp.concatenate([jnp.zeros((LEFT, D), values.dtype), values], 0)

    def one_block(start):
        query_rows = lax.dynamic_slice_in_dim(queries, start, block, 0).astype(jnp.float32).reshape(block, HEADS, head_width)
        key_rows = lax.dynamic_slice_in_dim(keys_padded, start, LEFT + block, 0).astype(jnp.float32).reshape(LEFT + block, HEADS, head_width)
        value_rows = lax.dynamic_slice_in_dim(values_padded, start, LEFT + block, 0).astype(jnp.float32).reshape(LEFT + block, HEADS, head_width)
        first = lax.dynamic_slice_in_dim(segment_edges[0], start, block, 0)
        last = lax.dynamic_slice_in_dim(segment_edges[1], start, block, 0)
        places = start - LEFT + jnp.arange(LEFT + block, dtype=jnp.int32)
        lower = jnp.maximum(first - LEFT, 0)
        visible = (places[None, :] >= lower[:, None]) & (places[None, :] <= last[:, None])
        scores = jnp.einsum('qhd,khd->hqk', query_rows, key_rows) * scale
        scores = jnp.where(visible[None], scores, -jnp.inf)
        highest = lax.optimization_barrier(jnp.max(scores, -1, keepdims=True))
        expos = jnp.exp(scores - highest)
        weights = (expos / lax.optimization_barrier(jnp.sum(expos, -1, keepdims=True))).astype(jnp.bfloat16)
        mixed = jnp.einsum('hqk,khd->qhd', weights.astype(jnp.float32), value_rows)
        return mixed.reshape(block, D).astype(jnp.bfloat16)
    starts = jnp.arange(total // block, dtype=jnp.int32) * block
    return lax.map(one_block, starts).reshape(total, D)

def reference(frames_in, queries, keys, values, segment_edges, out_proj, expert_ids, gates, w_gate, w_up, w_down):
    context = attend(queries, keys, values, segment_edges)
    attended = jnp.dot(context, out_proj, preferred_element_type=jnp.float32)
    hidden_state = (frames_in.astype(jnp.float32) + attended).astype(jnp.bfloat16)
    hidden_state = lax.optimization_barrier(hidden_state)
    state = hidden_state.astype(jnp.float32)
    normed = (state * lax.rsqrt(lax.optimization_barrier(jnp.mean(state * state, -1, keepdims=True)) + EPS)).astype(jnp.bfloat16)
    grouped = expert_ids.reshape(N_TM, F_DEV * TOP)
    onehot = (grouped[:, :, None] == jnp.arange(EXPERTS, dtype=jnp.int32)[None, None, :]).astype(jnp.int32)
    ranks = jnp.cumsum(onehot, 1) - onehot
    slots = lax.optimization_barrier(jnp.sum(ranks * onehot, -1))
    sources = jnp.arange(N_TM, dtype=jnp.int32)[:, None]
    targets = ((grouped * N_TM + sources) * CAP + slots).reshape(-1).astype(jnp.int32)
    owners = jnp.arange(FRAMES * TOP, dtype=jnp.int32) // TOP
    table = jnp.full((EXPERTS * N_TM * CAP,), FRAMES, jnp.int32).at[targets].set(owners)
    padded = jnp.concatenate([normed, jnp.zeros((1, D), jnp.bfloat16)], 0)
    buffers = padded[table].reshape(EXPERTS, N_TM * CAP, D)

    def expert(operands):
        rows_in, gate_weight, up_weight, down_weight = operands
        gate_act = jnp.dot(rows_in, gate_weight, preferred_element_type=jnp.float32)
        up_act = jnp.dot(rows_in, up_weight, preferred_element_type=jnp.float32)
        activity = (jax.nn.silu(gate_act) * up_act).astype(jnp.bfloat16)
        return jnp.dot(activity, down_weight, preferred_element_type=jnp.float32)
    results = lax.map(expert, (buffers, w_gate, w_up, w_down))
    picked = results.reshape(-1, D)[targets].reshape(FRAMES, TOP, D)
    mixture = lax.optimization_barrier(jnp.sum(gates[:, :, None] * picked, 1))
    return (state + mixture).astype(jnp.bfloat16)
```

```python
import functools

import jax
import jax.numpy as jnp
from jax import lax
from jax.experimental import pallas as pl
from jax.experimental.pallas import tpu as pltpu
from jax.sharding import PartitionSpec as P

HEADS = 16
LEFT = 256
EPS = 1e-06
NX = 4
NY = 4
QB = 128
MESH = pl.DeviceIdType.MESH
NEG = -1e30
BF = jnp.bfloat16
F32 = jnp.float32


def kernel(
    n_tm,
    cap,
    edges_ref,
    ids_ref,
    gates_ref,
    q_ref,
    k_hbm,
    v_hbm,
    f_hbm,
    wo_hbm,
    wg_hbm,
    wu_hbm,
    wd_hbm,
    out_ref,
    kbuf,
    vbuf,
    fbuf,
    wo,
    wg,
    wu,
    wd,
    ctx,
    hid,
    onehot,
    comb_hi,
    comb_lo,
    sbuf,
    xbuf,
    abuf,
    pown,
    psend,
    precv,
    q2,
    r2,
    q1,
    r1,
    hsend,
    rbuf,
    acc,
    loc_sem,
    halo_s,
    halo_r,
    wo_s,
    wo_r,
    c_s,
    c_r,
    d_s,
    d_r,
    e_s,
    e_r,
    g_s,
    g_r,
    h_s,
    h_r,
):
    t = lax.axis_index("tm")
    m = lax.axis_index("mp")
    nz = n_tm // NY
    y, z = t // nz, t % nz
    x, c = m // 2, m % 2
    x_r, x_l, x_o = (x + 1) % NX, (x + NX - 1) % NX, (x + 2) % NX
    m_r, m_l, m_o, m_s = x_r * 2 + c, x_l * 2 + c, x_o * 2 + c, x * 2 + 1 - c
    frames = q_ref.shape[0]
    n_exp = 2 * n_tm
    rc = nz * cap
    nxt, prv = (t + 1) % n_tm, (t + n_tm - 1) % n_tm

    def col(i):
        return pl.ds(pl.multiple_of(i * 128, 128), 128)

    def remote(src, dst, ss, rs, **dev):
        return pltpu.make_async_remote_copy(
            src_ref=src, dst_ref=dst, send_sem=ss, recv_sem=rs, device_id=dev, device_id_type=MESH
        )

    barrier = pltpu.get_barrier_semaphore()

    @pl.loop(1, n_tm)
    def _(i):
        pl.semaphore_signal(barrier, inc=1, device_id={"tm": (t + i) % n_tm}, device_id_type=MESH)

    @pl.loop(1, 2 * NX)
    def _(i):
        pl.semaphore_signal(barrier, inc=1, device_id={"mp": (m + i) % (2 * NX)}, device_id_type=MESH)

    own_k = pltpu.make_async_copy(k_hbm, kbuf.at[pl.ds(LEFT, frames)], loc_sem.at[0])
    own_v = pltpu.make_async_copy(v_hbm, vbuf.at[pl.ds(LEFT, frames)], loc_sem.at[1])
    own_f = pltpu.make_async_copy(f_hbm.at[:, col(m)], fbuf, loc_sem.at[2])
    own_o = pltpu.make_async_copy(
        wo_hbm.at[:, col(m)], wo.at[pl.ds(pl.multiple_of(m * 128, 128), 128)], loc_sem.at[3]
    )
    own_g = pltpu.make_async_copy(wg_hbm, wg, loc_sem.at[4])
    own_u = pltpu.make_async_copy(wu_hbm, wu, loc_sem.at[5])
    own_d = pltpu.make_async_copy(wd_hbm, wd, loc_sem.at[6])
    for copy in (own_k, own_v, own_f, own_o, own_g, own_u, own_d):
        copy.start()

    pl.semaphore_wait(barrier, n_tm - 1 + 2 * NX - 1)

    halo_k = remote(
        k_hbm.at[pl.ds(frames - LEFT, LEFT)], kbuf.at[pl.ds(0, LEFT)], halo_s.at[0], halo_r.at[0], tm=nxt
    )
    halo_v = remote(
        v_hbm.at[pl.ds(frames - LEFT, LEFT)], vbuf.at[pl.ds(0, LEFT)], halo_s.at[1], halo_r.at[1], tm=nxt
    )
    halo_k.start()
    halo_v.start()

    def wo_copy(i):
        peer = (m + i) % (2 * NX)
        return remote(
            wo_hbm.at[:, col(peer)],
            wo.at[pl.ds(pl.multiple_of(m * 128, 128), 128)],
            wo_s.at[i],
            wo_r.at[i],
            mp=peer,
        )

    @pl.loop(1, 2 * NX)
    def _(i):
        wo_copy(i).start()

    scale = (wo_hbm.shape[1] // HEADS) ** (-0.5)
    head = wo_hbm.shape[1] // HEADS
    lane = lax.broadcasted_iota(jnp.int32, (QB, 128), 1)
    win = LEFT + QB

    def attend(b):
        rows = pl.ds(pl.multiple_of(b * QB, QB), QB)
        keys = pl.ds(pl.multiple_of(b * QB, QB), win)
        q = q_ref[rows, :].astype(F32) * scale
        q_both = jnp.concatenate(
            [jnp.where(lane < head, q, 0.0), jnp.where(lane >= head, q, 0.0)], 0
        ).astype(BF)
        s = lax.dot_general(
            kbuf[keys, :], q_both, (((1,), (1,)), ((), ())), preferred_element_type=F32
        )
        lower = jnp.maximum(edges_ref[0:1, rows] - LEFT, 0)
        upper = edges_ref[1:2, rows]
        lower = jnp.concatenate([lower, lower], 1)
        upper = jnp.concatenate([upper, upper], 1)
        place = lax.broadcasted_iota(jnp.int32, (win, 2 * QB), 0) + (t * frames - LEFT + b * QB)
        s = jnp.where((place >= lower) & (place <= upper), s, NEG)
        p = jnp.exp(s - jnp.max(s, 0, keepdims=True))
        total = jnp.sum(p, 0, keepdims=True)
        v_t = vbuf[keys, :].astype(F32).T.astype(BF)
        o = jnp.dot(v_t, p.astype(BF), preferred_element_type=F32) / total
        both = jnp.concatenate([o[:head, :QB], o[head:, QB:]], 0)
        ctx[rows, col(m)] = both.T.astype(BF)

    half = frames // 2

    def c_rows(r):
        return pl.ds(pl.multiple_of(r * half, half), half)

    def c_half(r, h):
        return pl.ds(pl.multiple_of(r * half + h * (half // 2), half // 2), half // 2)

    def cx(r, k, rows, blk, dev):
        ref = ctx.at[rows, col(blk)]
        return remote(ref, ref, c_s.at[r, k], c_r.at[r, k], mp=dev)

    def c1(r):
        cx(r, 0, c_rows(r), m, m_r).start()
        cx(r, 1, c_rows(r), m, m_l).start()
        cx(r, 4, c_rows(r), m, m_s).start()

    def c2(r):
        cx(r, 0, c_rows(r), m_l, m_r).wait_recv()
        cx(r, 2, c_half(r, 0), m_l, m_r).start()
        cx(r, 1, c_rows(r), m_r, m_l).wait_recv()
        cx(r, 3, c_half(r, 1), m_r, m_l).start()
        cx(r, 5, c_rows(r), m_l, m_s).start()
        cx(r, 6, c_rows(r), m_r, m_s).start()

    def other(i):
        return i + 1 - 2 * c

    def c3(r):
        cx(r, 2, c_half(r, 0), m_o, m_r).wait_recv()
        cx(r, 3, c_half(r, 1), m_o, m_l).wait_recv()
        cx(r, 7, c_rows(r), m_o, m_s).start()
        cx(r, 4, c_rows(r), other(m), m_s).wait_recv()
        cx(r, 5, c_rows(r), other(m_l), m_s).wait_recv()
        cx(r, 6, c_rows(r), other(m_r), m_s).wait_recv()
        cx(r, 7, c_rows(r), other(m_o), m_s).wait_recv()

    def c_sent(r):
        cx(r, 0, c_rows(r), m, m_r).wait_send()
        cx(r, 1, c_rows(r), m, m_l).wait_send()
        cx(r, 2, c_half(r, 0), m_l, m_r).wait_send()
        cx(r, 3, c_half(r, 1), m_r, m_l).wait_send()
        cx(r, 4, c_rows(r), m, m_s).wait_send()
        cx(r, 5, c_rows(r), m_l, m_s).wait_send()
        cx(r, 6, c_rows(r), m_r, m_s).wait_send()
        cx(r, 7, c_rows(r), m_o, m_s).wait_send()

    own_k.wait()
    own_v.wait()
    per_half = half // QB

    @pl.loop(per_half, 2 * per_half)
    def _(b):
        attend(b)

    c1(1)
    halo_k.wait_recv()
    halo_v.wait_recv()

    @pl.loop(0, per_half)
    def _(b):
        attend(b)

    c1(0)
    c2(1)

    id0, id1 = ids_ref[0:1, :], ids_ref[1:2, :]
    e_iota = lax.broadcasted_iota(jnp.int32, (n_exp, frames), 0)
    is0, is1 = e_iota == id0, e_iota == id1
    named = jnp.where(is0 | is1, 1.0, 0.0).astype(BF)
    before = jnp.where(
        lax.broadcasted_iota(jnp.int32, (frames, frames), 0)
        < lax.broadcasted_iota(jnp.int32, (frames, frames), 1),
        1.0,
        0.0,
    ).astype(BF)
    ranks = jnp.dot(named, before, preferred_element_type=F32)
    slot0 = jnp.sum(jnp.where(is0, ranks, 0.0), 0, keepdims=True).astype(jnp.int32)
    slot1 = jnp.sum(jnp.where(is1, ranks, 0.0), 0, keepdims=True).astype(jnp.int32)
    tgt0, tgt1 = id0 * cap + slot0, id1 * cap + slot1

    @pl.loop(0, n_exp * cap // 128)
    def _(i):
        rows = pl.ds(pl.multiple_of(i * 128, 128), 128)
        place = lax.broadcasted_iota(jnp.int32, (128, frames), 0) + i * 128
        onehot[rows, :] = jnp.where((place == tgt0) | (place == tgt1), 1.0, 0.0).astype(BF)

    c3(1)
    c2(0)

    @pl.loop(1, 2 * NX)
    def _(i):
        wo_copy(i).wait_recv()

    own_o.wait()
    own_f.wait()

    def hidden(r):
        rows = c_rows(r)
        hid[rows, :] = (
            fbuf[rows, :].astype(F32) + jnp.dot(ctx[rows, :], wo[...], preferred_element_type=F32)
        ).astype(BF)

    hidden(1)
    c3(0)
    hidden(0)

    def d_copy(ty, i):
        d = ty * nz + (z + i) % nz
        return remote(
            sbuf.at[d],
            xbuf.at[:, pl.ds(pl.multiple_of(t * cap, cap), cap), col(m)],
            d_s.at[d],
            d_r.at[t],
            tm=d,
        )

    def d_own():
        return pltpu.make_async_copy(
            sbuf.at[t],
            xbuf.at[:, pl.ds(pl.multiple_of(t * cap, cap), cap), col(m)],
            d_r.at[t],
        )

    def d_wait(src):
        return remote(
            sbuf.at[src],
            xbuf.at[:, pl.ds(pl.multiple_of(src * cap, cap), cap), col(m)],
            d_s.at[src],
            d_r.at[src],
            tm=src,
        )

    @pl.loop(0, NY)
    def _(j):
        ty = (y + NY - j) % NY
        rows = pl.ds(pl.multiple_of(ty * (2 * rc), 2 * rc), 2 * rc)
        sent = jnp.dot(onehot[rows, :], hid[...], preferred_element_type=F32)
        sbuf[pl.ds(ty * nz, nz)] = sent.astype(BF).reshape(nz, 2, cap, 128)

        @pl.loop(0, nz)
        def _(i):
            stays = (j == 0) & (i == 0)

            @pl.when(stays)
            def _():
                d_own().start()

            @pl.when(jnp.logical_not(stays))
            def _():
                d_copy(ty, i).start()

    g0, g1 = gates_ref[0:1, :], gates_ref[1:2, :]
    g0_hi, g1_hi = g0.astype(BF).astype(F32), g1.astype(BF).astype(F32)
    g0_lo, g1_lo = g0 - g0_hi, g1 - g1_hi

    @pl.loop(0, n_exp * cap // 128)
    def _(i):
        rows = pl.ds(pl.multiple_of(i * 128, 128), 128)
        place = lax.broadcasted_iota(jnp.int32, (128, frames), 0) + i * 128
        at0, at1 = place == tgt0, place == tgt1
        comb_hi[rows, :] = jnp.where(at0, g0_hi, jnp.where(at1, g1_hi, 0.0)).astype(BF)
        comb_lo[rows, :] = jnp.where(at0, g0_lo, jnp.where(at1, g1_lo, 0.0)).astype(BF)

    def src_y(j):
        return (y + j) % NY

    def e_rows(j):
        return pl.ds(pl.multiple_of(src_y(j) * rc, rc), rc)

    def ex(j, k, ref, dev):
        return remote(ref, ref, e_s.at[j, k], e_r.at[j, k], mp=dev)

    def e_blk(j, blk):
        return xbuf.at[:, e_rows(j), col(blk)]

    def e_half(j, h, blk):
        return xbuf.at[h, e_rows(j), col(blk)]

    def e1(j):
        @pl.loop(0, nz)
        def _(i):
            stays = (j == 0) & (i == 0)

            @pl.when(stays)
            def _():
                d_own().wait()

            @pl.when(jnp.logical_not(stays))
            def _():
                d_wait(src_y(j) * nz + (z + nz - i) % nz).wait_recv()

        ex(j, 0, e_blk(j, m), m_r).start()
        ex(j, 1, e_blk(j, m), m_l).start()
        ex(j, 4, e_blk(j, m), m_s).start()

    def e2(j):
        ex(j, 0, e_blk(j, m_l), m_r).wait_recv()
        ex(j, 2, e_half(j, 0, m_l), m_r).start()
        ex(j, 1, e_blk(j, m_r), m_l).wait_recv()
        ex(j, 3, e_half(j, 1, m_r), m_l).start()
        ex(j, 5, e_blk(j, m_l), m_s).start()
        ex(j, 6, e_blk(j, m_r), m_s).start()

    def e3(j):
        ex(j, 2, e_half(j, 0, m_o), m_r).wait_recv()
        ex(j, 3, e_half(j, 1, m_o), m_l).wait_recv()
        ex(j, 7, e_blk(j, m_o), m_s).start()

    def e4(j):
        ex(j, 4, e_blk(j, other(m)), m_s).wait_recv()
        ex(j, 5, e_blk(j, other(m_l)), m_s).wait_recv()
        ex(j, 6, e_blk(j, other(m_r)), m_s).wait_recv()
        ex(j, 7, e_blk(j, other(m_o)), m_s).wait_recv()

    def e_sent(j):
        ex(j, 0, e_blk(j, m), m_r).wait_send()
        ex(j, 1, e_blk(j, m), m_l).wait_send()
        ex(j, 2, e_half(j, 0, m_l), m_r).wait_send()
        ex(j, 3, e_half(j, 1, m_r), m_l).wait_send()
        ex(j, 4, e_blk(j, m), m_s).wait_send()
        ex(j, 5, e_blk(j, m_l), m_s).wait_send()
        ex(j, 6, e_blk(j, m_r), m_s).wait_send()
        ex(j, 7, e_blk(j, m_o), m_s).wait_send()

    def g_sib(j, e):
        return remote(psend.at[j, e], precv.at[j, e], g_s.at[j, e], g_r.at[j, e], mp=m_s)

    def g_far(j, h, dev):
        return remote(q2.at[j, h], r2.at[j, h], g_s.at[j, 2 + h], g_r.at[j, 2 + h], mp=dev)

    def g_near(j, h, dev):
        return remote(q1.at[j, h], r1.at[j, h], g_s.at[j, 4 + h], g_r.at[j, 4 + h], mp=dev)

    def experts(j):
        rows = e_rows(j)

        @pl.loop(0, 2)
        def _(e):
            v = xbuf[e, rows, :].astype(F32)
            inv = lax.rsqrt(jnp.mean(v * v, 1, keepdims=True) + EPS)
            normed = (v * inv).astype(BF)
            g = jnp.dot(normed, wg[e], preferred_element_type=F32)
            u = jnp.dot(normed, wu[e], preferred_element_type=F32)
            a = (g / (1.0 + jnp.exp(-g)) * u).astype(BF)
            abuf[...] = a
            w_far = jnp.concatenate([wd[e, :, col(i * 2 + 1 - c)] for i in range(NX)], 1)
            o_far = jnp.dot(abuf[...], w_far, preferred_element_type=F32).astype(BF)
            for i in range(NX):
                psend[j, e, i] = o_far[:, i * 128 : (i + 1) * 128]
            g_sib(j, e).start()
            w_own = jnp.concatenate([wd[e, :, col(i * 2 + c)] for i in range(NX)], 1)
            o_own = jnp.dot(abuf[...], w_own, preferred_element_type=F32)
            for i in range(NX):
                pown[j, e, i] = o_own[:, i * 128 : (i + 1) * 128]

    def both(j, e, blk):
        return pown[j, e, blk] + precv[j, e, blk].astype(F32)

    def g1(j):
        g_sib(j, 0).wait_recv()
        q2[j, 0] = both(j, 0, x_o).astype(BF)
        g_far(j, 0, m_r).start()
        g_sib(j, 1).wait_recv()
        q2[j, 1] = both(j, 1, x_o).astype(BF)
        g_far(j, 1, m_l).start()

    def g2(j):
        q1[j, 0, 1] = both(j, 1, x_r).astype(BF)
        q1[j, 1, 0] = both(j, 0, x_l).astype(BF)
        g_far(j, 0, m_r).wait_recv()
        q1[j, 0, 0] = (both(j, 0, x_r) + r2[j, 0].astype(F32)).astype(BF)
        g_near(j, 0, m_r).start()
        g_far(j, 1, m_l).wait_recv()
        q1[j, 1, 1] = (both(j, 1, x_l) + r2[j, 1].astype(F32)).astype(BF)
        g_near(j, 1, m_l).start()

    def h_copy(j, i):
        d = src_y(j) * nz + (z + nz - i) % nz
        return remote(
            hsend.at[j, :, pl.ds(pl.multiple_of((d % nz) * cap, cap), cap), :],
            rbuf.at[t],
            h_s.at[d],
            h_r.at[t],
            tm=d,
        )

    def h_own():
        return pltpu.make_async_copy(
            hsend.at[0, :, pl.ds(pl.multiple_of(z * cap, cap), cap), :], rbuf.at[t], h_r.at[t]
        )

    def h_wait(src):
        return remote(rbuf.at[src], rbuf.at[src], h_s.at[src], h_r.at[src], tm=src)

    def g3(j):
        g_near(j, 0, m_r).wait_recv()
        g_near(j, 1, m_l).wait_recv()
        for e in range(2):
            hsend[j, e] = (
                both(j, e, x) + r1[j, 0, e].astype(F32) + r1[j, 1, e].astype(F32)
            ).astype(BF)

        @pl.loop(0, nz)
        def _(i):
            stays = (j == 0) & (i == 0)

            @pl.when(stays)
            def _():
                h_own().start()

            @pl.when(jnp.logical_not(stays))
            def _():
                h_copy(j, i).start()

    def g_sent(j):
        for e in range(2):
            g_sib(j, e).wait_send()
        g_far(j, 0, m_r).wait_send()
        g_far(j, 1, m_l).wait_send()
        g_near(j, 0, m_r).wait_send()
        g_near(j, 1, m_l).wait_send()

    own_g.wait()
    own_u.wait()
    own_d.wait()

    def stage(k, f):
        @pl.when((k >= 0) & (k < NY))
        def _():
            f(k)

    @pl.loop(0, NY + 5)
    def _(tick):
        stage(tick - 1, e2)
        stage(tick, e1)
        stage(tick - 2, e3)
        stage(tick - 5, g3)
        stage(tick - 4, g2)
        stage(tick - 3, g1)
        stage(tick - 2, e4)
        stage(tick - 2, experts)

    acc[...] = jnp.zeros_like(acc)

    @pl.loop(0, NY)
    def _(j):
        oy = (y + NY - j) % NY

        @pl.loop(0, nz)
        def _(i):
            stays = (j == 0) & (i == 0)

            @pl.when(stays)
            def _():
                h_own().wait()

            @pl.when(jnp.logical_not(stays))
            def _():
                h_wait(oy * nz + (z + i) % nz).wait_recv()

        rows = pl.ds(pl.multiple_of(oy * (2 * rc), 2 * rc), 2 * rc)
        back = rbuf[pl.ds(oy * nz, nz)].reshape(2 * rc, 128)
        back_t = back.astype(F32).T.astype(BF)
        acc[...] += jnp.dot(back_t, comb_hi[rows, :], preferred_element_type=F32) + jnp.dot(
            back_t, comb_lo[rows, :], preferred_element_type=F32
        )

    out_ref[...] = (hid[...].astype(F32) + acc[...].T).astype(BF)

    halo_k.wait_send()
    halo_v.wait_send()

    @pl.loop(1, 2 * NX)
    def _(i):
        wo_copy(i).wait_send()

    @pl.loop(0, 2)
    def _(r):
        c_sent(r)

    @pl.loop(0, NY)
    def _(j):
        e_sent(j)
        g_sent(j)

        @pl.loop(0, nz)
        def _(i):
            stays = (j == 0) & (i == 0)

            @pl.when(jnp.logical_not(stays))
            def _():
                d_copy((y + NY - j) % NY, i).wait_send()
                h_copy(j, i).wait_send()


def per_device(
    frames_in,
    queries,
    keys,
    values,
    segment_edges,
    out_proj,
    expert_ids,
    gates,
    w_gate,
    w_up,
    w_down,
):
    frames = frames_in.shape[0]
    n_tm = lax.axis_size("tm")
    model = frames_in.shape[1]
    inner = w_gate.shape[2]
    n_exp = w_gate.shape[0] * n_tm
    cap = 4 * frames // n_exp
    rc = n_tm // NY * cap
    slots = n_exp * cap
    vmem = pl.BlockSpec(memory_space=pltpu.VMEM)
    anyw = pl.BlockSpec(memory_space=pl.ANY)
    dma = pltpu.SemaphoreType.DMA
    return pl.pallas_call(
        functools.partial(kernel, n_tm, cap),
        out_shape=jax.ShapeDtypeStruct((frames, 128), BF),
        in_specs=[vmem] * 4 + [anyw] * 7,
        out_specs=vmem,
        scratch_shapes=[
            pltpu.VMEM((LEFT + frames, 128), BF),
            pltpu.VMEM((LEFT + frames, 128), BF),
            pltpu.VMEM((frames, 128), BF),
            pltpu.VMEM((model, 128), BF),
            pltpu.VMEM(w_gate.shape, BF),
            pltpu.VMEM(w_up.shape, BF),
            pltpu.VMEM(w_down.shape, BF),
            pltpu.VMEM((frames, model), BF),
            pltpu.VMEM((frames, 128), BF),
            pltpu.VMEM((slots, frames), BF),
            pltpu.VMEM((slots, frames), BF),
            pltpu.VMEM((slots, frames), BF),
            pltpu.VMEM((n_tm, 2, cap, 128), BF),
            pltpu.VMEM((2, n_tm * cap, model), BF),
            pltpu.VMEM((rc, inner), BF),
            pltpu.VMEM((NY, 2, NX, rc, 128), F32),
            pltpu.VMEM((NY, 2, NX, rc, 128), BF),
            pltpu.VMEM((NY, 2, NX, rc, 128), BF),
            pltpu.VMEM((NY, 2, rc, 128), BF),
            pltpu.VMEM((NY, 2, rc, 128), BF),
            pltpu.VMEM((NY, 2, 2, rc, 128), BF),
            pltpu.VMEM((NY, 2, 2, rc, 128), BF),
            pltpu.VMEM((NY, 2, rc, 128), BF),
            pltpu.VMEM((n_tm, 2, cap, 128), BF),
            pltpu.VMEM((128, frames), F32),
            dma((7,)),
            dma((2,)),
            dma((2,)),
            dma((2 * NX,)),
            dma((2 * NX,)),
            dma((2, 8)),
            dma((2, 8)),
            dma((n_tm,)),
            dma((n_tm,)),
            dma((NY, 8)),
            dma((NY, 8)),
            dma((NY, 6)),
            dma((NY, 6)),
            dma((n_tm,)),
            dma((n_tm,)),
        ],
        compiler_params=pltpu.CompilerParams(
            collective_id=0, has_side_effects=True, vmem_limit_bytes=56 * 1024 * 1024
        ),
        name="layer",
    )(
        segment_edges,
        expert_ids.T,
        gates.T,
        queries,
        keys,
        values,
        frames_in,
        out_proj,
        w_gate,
        w_up,
        w_down,
    )


def solution(mesh):
    return jax.shard_map(
        per_device,
        mesh=mesh,
        in_specs=(
            P("tm", None),
            P("tm", "mp"),
            P("tm", "mp"),
            P("tm", "mp"),
            P(None, "tm"),
            P("mp", None),
            P("tm", None),
            P("tm", None),
            P("tm", None, "mp"),
            P("tm", None, "mp"),
            P("tm", "mp", None),
        ),
        out_specs=P("tm", "mp"),
        check_vma=False,
    )
```

```python
import functools

import jax
import jax.numpy as jnp
from jax import lax
from jax.experimental import pallas as pl
from jax.experimental.pallas import tpu as pltpu
from jax.sharding import PartitionSpec as P

HEADS = 16
LEFT = 256
EPS = 1e-06
NX = 4
NY = 4
QB = 128
PARTS = 4
AHEAD = (0, 2, 4, 5, 7, 9, 11)
ORDER = (0, 1, 2, 4, 5, 6, 3)
MESH = pl.DeviceIdType.MESH
NEG = -1e30
BF = jnp.bfloat16
F32 = jnp.float32


def relative_order(nz, parts):
    cells = sorted(
        ((dy, dz) for dy in range(NY) for dz in range(nz)),
        key=lambda o: min(o[0], NY - o[0]) + min(o[1], nz - o[1]),
    )
    size = len(cells) // parts
    groups = [cells[i * size : (i + 1) * size] for i in range(parts)]
    return sum(groups[::2] + groups[1::2][::-1], [])


def kernel(
    n_tm,
    cap,
    parts,
    edges_ref,
    ids_ref,
    gates_ref,
    q_ref,
    k_hbm,
    v_hbm,
    f_hbm,
    wo_hbm,
    wg_hbm,
    wu_hbm,
    wd_hbm,
    out_ref,
    kbuf,
    vbuf,
    fbuf,
    wo,
    wg,
    wu,
    wd,
    ctx,
    hid,
    onehot,
    comb_hi,
    comb_lo,
    sbuf,
    xbuf,
    abuf,
    pown,
    psend,
    precv,
    q2,
    r2,
    q1,
    r1,
    hsend,
    rbuf,
    acc,
    loc_sem,
    halo_s,
    halo_r,
    wo_s,
    wo_r,
    c_s,
    c_r,
    d_s,
    d_r,
    e_s,
    e_r,
    g_s,
    g_r,
    h_s,
    h_r,
    know,
):
    t = lax.axis_index("tm")
    m = lax.axis_index("mp")
    nz = n_tm // NY
    y, z = t // nz, t % nz
    x, c = m // 2, m % 2
    x_r, x_l, x_o = (x + 1) % NX, (x + NX - 1) % NX, (x + 2) % NX
    m_r, m_l, m_o, m_s = x_r * 2 + c, x_l * 2 + c, x_o * 2 + c, x * 2 + 1 - c
    frames = q_ref.shape[0]
    n_exp = 2 * n_tm
    per = n_tm // parts
    rc = per * cap
    chunks = 2 * parts
    offsets = relative_order(nz, parts)
    nxt, prv = (t + 1) % n_tm, (t + n_tm - 1) % n_tm

    def col(i):
        return pl.ds(pl.multiple_of(i * 128, 128), 128)

    def remote(src, dst, ss, rs, **dev):
        return pltpu.make_async_remote_copy(
            src_ref=src, dst_ref=dst, send_sem=ss, recv_sem=rs, device_id=dev, device_id_type=MESH
        )

    barrier = pltpu.get_barrier_semaphore()

    def tell(sem, dy, dz):
        pl.semaphore_signal(
            sem, inc=1, device_id={"tm": (y + dy) % NY * nz + (z + dz) % nz}, device_id_type=MESH
        )

    for dy in range(1, NY):
        tell(barrier, dy, 0)
    if nz > 1:
        tell(barrier, 0, 1)
        tell(barrier, 0, nz - 1)
    for peer in (nxt, prv):
        pl.semaphore_signal(barrier, inc=1, device_id={"tm": peer}, device_id_type=MESH)

    @pl.loop(1, 2 * NX)
    def _(i):
        pl.semaphore_signal(barrier, inc=1, device_id={"mp": (m + i) % (2 * NX)}, device_id_type=MESH)

    own_k = pltpu.make_async_copy(k_hbm, kbuf.at[pl.ds(LEFT, frames)], loc_sem.at[0])
    own_v = pltpu.make_async_copy(v_hbm, vbuf.at[pl.ds(LEFT, frames)], loc_sem.at[1])
    own_f = pltpu.make_async_copy(f_hbm.at[:, col(m)], fbuf, loc_sem.at[2])
    own_o = pltpu.make_async_copy(
        wo_hbm.at[:, col(m)], wo.at[pl.ds(pl.multiple_of(m * 128, 128), 128)], loc_sem.at[3]
    )
    own_g = pltpu.make_async_copy(wg_hbm, wg, loc_sem.at[4])
    own_u = pltpu.make_async_copy(wu_hbm, wu, loc_sem.at[5])
    own_d = pltpu.make_async_copy(wd_hbm, wd, loc_sem.at[6])
    for copy in (own_k, own_v, own_f, own_o, own_g, own_u, own_d):
        copy.start()

    halo_k = remote(
        k_hbm.at[pl.ds(frames - LEFT, LEFT)], kbuf.at[pl.ds(0, LEFT)], halo_s.at[0], halo_r.at[0], tm=nxt
    )
    halo_v = remote(
        v_hbm.at[pl.ds(frames - LEFT, LEFT)], vbuf.at[pl.ds(0, LEFT)], halo_s.at[1], halo_r.at[1], tm=nxt
    )

    def wo_copy(i):
        peer = (m + i) % (2 * NX)
        return remote(
            wo_hbm.at[:, col(peer)],
            wo.at[pl.ds(pl.multiple_of(m * 128, 128), 128)],
            wo_s.at[i],
            wo_r.at[i],
            mp=peer,
        )

    scale = (wo_hbm.shape[1] // HEADS) ** (-0.5)
    head = wo_hbm.shape[1] // HEADS
    lane = lax.broadcasted_iota(jnp.int32, (QB, 128), 1)
    win = LEFT + QB

    def attend(b):
        rows = pl.ds(pl.multiple_of(b * QB, QB), QB)
        keys = pl.ds(pl.multiple_of(b * QB, QB), win)
        q = q_ref[rows, :].astype(F32) * scale
        q_both = jnp.concatenate(
            [jnp.where(lane < head, q, 0.0), jnp.where(lane >= head, q, 0.0)], 0
        ).astype(BF)
        s = lax.dot_general(
            kbuf[keys, :], q_both, (((1,), (1,)), ((), ())), preferred_element_type=F32
        )
        lower = jnp.maximum(edges_ref[0:1, rows] - LEFT, 0)
        upper = edges_ref[1:2, rows]
        lower = jnp.concatenate([lower, lower], 1)
        upper = jnp.concatenate([upper, upper], 1)
        place = lax.broadcasted_iota(jnp.int32, (win, 2 * QB), 0) + (t * frames - LEFT + b * QB)
        s = jnp.where((place >= lower) & (place <= upper), s, NEG)
        p = jnp.exp(s - jnp.max(s, 0, keepdims=True))
        total = jnp.sum(p, 0, keepdims=True)
        v_t = vbuf[keys, :].astype(F32).T.astype(BF)
        o = jnp.dot(v_t, p.astype(BF), preferred_element_type=F32) / total
        both = jnp.concatenate([o[:head, :QB], o[head:, QB:]], 0)
        ctx[rows, col(m)] = both.T.astype(BF)

    half = frames // 2

    def c_rows(r):
        return pl.ds(pl.multiple_of(r * half, half), half)

    def cx(r, k, rows, blk, dev):
        ref = ctx.at[rows, col(blk)]
        return remote(ref, ref, c_s.at[r, k], c_r.at[r, k], mp=dev)

    def c1(r):
        cx(r, 0, c_rows(r), m, m_r).start()
        cx(r, 1, c_rows(r), m, m_l).start()
        cx(r, 2, c_rows(r), m, m_o).start()
        cx(r, 3, c_rows(r), m, m_s).start()

    def other(i):
        return i + 1 - 2 * c

    def c2(r):
        cx(r, 0, c_rows(r), m_l, m_r).wait_recv()
        cx(r, 4, c_rows(r), m_l, m_s).start()
        cx(r, 1, c_rows(r), m_r, m_l).wait_recv()
        cx(r, 5, c_rows(r), m_r, m_s).start()
        cx(r, 2, c_rows(r), m_o, m_o).wait_recv()
        cx(r, 6, c_rows(r), m_o, m_s).start()

    def c3(r):
        cx(r, 3, c_rows(r), other(m), m_s).wait_recv()
        cx(r, 4, c_rows(r), other(m_l), m_s).wait_recv()
        cx(r, 5, c_rows(r), other(m_r), m_s).wait_recv()
        cx(r, 6, c_rows(r), other(m_o), m_s).wait_recv()

    def c_sent(r):
        cx(r, 0, c_rows(r), m, m_r).wait_send()
        cx(r, 1, c_rows(r), m, m_l).wait_send()
        cx(r, 2, c_rows(r), m, m_o).wait_send()
        cx(r, 3, c_rows(r), m, m_s).wait_send()
        cx(r, 4, c_rows(r), m_l, m_s).wait_send()
        cx(r, 5, c_rows(r), m_r, m_s).wait_send()
        cx(r, 6, c_rows(r), m_o, m_s).wait_send()

    own_k.wait()
    own_v.wait()
    per_half = half // QB

    @pl.loop(per_half, 2 * per_half)
    def _(b):
        attend(b)

    pl.semaphore_wait(barrier, NY - 1 + 2 * (nz > 1) + 2 + 2 * NX - 1)
    halo_k.start()
    halo_v.start()
    c1(1)

    @pl.loop(1, 2 * NX)
    def _(i):
        wo_copy(i).start()

    if nz > 1:
        tell(know.at[0], 0, 1)
        tell(know.at[0], 0, nz - 1)

    id0, id1 = ids_ref[0:1, :], ids_ref[1:2, :]
    e_iota = lax.broadcasted_iota(jnp.int32, (n_exp, frames), 0)
    is0, is1 = e_iota == id0, e_iota == id1
    named = jnp.where(is0 | is1, 1.0, 0.0).astype(BF)
    before = jnp.where(
        lax.broadcasted_iota(jnp.int32, (frames, frames), 0)
        < lax.broadcasted_iota(jnp.int32, (frames, frames), 1),
        1.0,
        0.0,
    ).astype(BF)
    ranks = jnp.dot(named, before, preferred_element_type=F32)
    slot0 = jnp.sum(jnp.where(is0, ranks, 0.0), 0, keepdims=True).astype(jnp.int32)
    slot1 = jnp.sum(jnp.where(is1, ranks, 0.0), 0, keepdims=True).astype(jnp.int32)
    owner = lax.broadcasted_iota(jnp.int32, (n_exp, frames), 0)
    first = jnp.zeros((n_exp, frames), jnp.int32)
    for p, (dy, dz) in enumerate(offsets):
        d = (y + NY - dy) % NY * nz + (z + nz - dz) % nz
        first = jnp.where((owner == 2 * d) | (owner == 2 * d + 1), (2 * p - 2 * d) * cap, first)
    first = first + owner * cap
    tgt0 = slot0 + jnp.sum(jnp.where(is0, first, 0), 0, keepdims=True)
    tgt1 = slot1 + jnp.sum(jnp.where(is1, first, 0), 0, keepdims=True)

    @pl.loop(0, n_exp * cap // 128)
    def _(i):
        rows = pl.ds(pl.multiple_of(i * 128, 128), 128)
        place = lax.broadcasted_iota(jnp.int32, (128, frames), 0) + i * 128
        onehot[rows, :] = jnp.where((place == tgt0) | (place == tgt1), 1.0, 0.0).astype(BF)

    if nz > 1:
        pl.semaphore_wait(know.at[0], 2)
        tell(know.at[1], 0, 2 % nz)
        tell(know.at[1], 0, nz - 2)
    c2(1)
    halo_k.wait_recv()
    halo_v.wait_recv()

    @pl.loop(0, per_half)
    def _(b):
        attend(b)

    c1(0)
    c3(1)
    if nz > 1:
        pl.semaphore_wait(know.at[1], 2)
    for dy in range(1, NY):
        tell(know.at[2], dy, 0)

    g0, g1 = gates_ref[0:1, :], gates_ref[1:2, :]
    g0_hi, g1_hi = g0.astype(BF).astype(F32), g1.astype(BF).astype(F32)
    g0_lo, g1_lo = g0 - g0_hi, g1 - g1_hi

    @pl.loop(0, n_exp * cap // 128)
    def _(i):
        rows = pl.ds(pl.multiple_of(i * 128, 128), 128)
        place = lax.broadcasted_iota(jnp.int32, (128, frames), 0) + i * 128
        at0, at1 = place == tgt0, place == tgt1
        comb_hi[rows, :] = jnp.where(at0, g0_hi, jnp.where(at1, g1_hi, 0.0)).astype(BF)
        comb_lo[rows, :] = jnp.where(at0, g0_lo, jnp.where(at1, g1_lo, 0.0)).astype(BF)

    @pl.loop(1, 2 * NX)
    def _(i):
        wo_copy(i).wait_recv()

    own_o.wait()
    own_f.wait()

    def hidden(r):
        rows = c_rows(r)
        hid[rows, :] = (
            fbuf[rows, :].astype(F32) + jnp.dot(ctx[rows, :], wo[...], preferred_element_type=F32)
        ).astype(BF)

    hidden(1)
    c2(0)
    c3(0)
    hidden(0)
    pl.semaphore_wait(know.at[2], NY - 1)

    def tm_at(p, sign):
        dy, dz = offsets[p]
        return (y + NY + sign * dy) % NY * nz + (z + nz + sign * dz) % nz

    def x_rows(p):
        return pl.ds(p * cap, cap)

    def d_copy(p):
        if p == 0:
            return pltpu.make_async_copy(sbuf.at[p], xbuf.at[:, x_rows(p), col(m)], d_r.at[p])
        return remote(
            sbuf.at[p], xbuf.at[:, x_rows(p), col(m)], d_s.at[p], d_r.at[p], tm=tm_at(p, -1)
        )

    def d_wait(p):
        if p == 0:
            d_copy(p).wait()
        else:
            d_copy(p).wait_recv()

    sent_rows = n_tm * 2 * cap // 4
    for i in range(4):
        sent = jnp.dot(
            onehot[i * sent_rows : (i + 1) * sent_rows, :], hid[...], preferred_element_type=F32
        )
        sbuf[i * n_tm // 4 : (i + 1) * n_tm // 4] = sent.astype(BF).reshape(n_tm // 4, 2, cap, 128)
        for p in range(i * n_tm // 4, (i + 1) * n_tm // 4):
            d_copy(p).start()

    def e_rows(j):
        return pl.ds(pl.multiple_of(j // 2 * rc, rc), rc)

    def ex(j, k, ref, dev):
        return remote(ref, ref, e_s.at[j, k], e_r.at[j, k], mp=dev)

    def e_blk(j, blk):
        return xbuf.at[j % 2, e_rows(j), col(blk)]

    def e_half(j, h, blk):
        rows = pl.ds(pl.multiple_of(j // 2 * rc + h * (rc // 2), rc // 2), rc // 2)
        return xbuf.at[j % 2, rows, col(blk)]

    def e1(j):
        for k in range(parts):

            @pl.when(j == 2 * k)
            def _(k=k):
                for p in range(k * per, (k + 1) * per):
                    d_wait(p)

        ex(j, 0, e_blk(j, m), m_r).start()
        ex(j, 1, e_blk(j, m), m_l).start()
        ex(j, 4, e_blk(j, m), m_s).start()

    def e2(j):
        ex(j, 0, e_blk(j, m_l), m_r).wait_recv()
        ex(j, 2, e_half(j, 0, m_l), m_r).start()
        ex(j, 1, e_blk(j, m_r), m_l).wait_recv()
        ex(j, 3, e_half(j, 1, m_r), m_l).start()
        ex(j, 5, e_blk(j, m_l), m_s).start()
        ex(j, 6, e_blk(j, m_r), m_s).start()

    def e3(j):
        ex(j, 2, e_half(j, 0, m_o), m_r).wait_recv()
        ex(j, 3, e_half(j, 1, m_o), m_l).wait_recv()
        ex(j, 7, e_blk(j, m_o), m_s).start()

    def e4(j):
        ex(j, 4, e_blk(j, other(m)), m_s).wait_recv()
        ex(j, 5, e_blk(j, other(m_l)), m_s).wait_recv()
        ex(j, 6, e_blk(j, other(m_r)), m_s).wait_recv()
        ex(j, 7, e_blk(j, other(m_o)), m_s).wait_recv()

    def e_sent(j):
        ex(j, 0, e_blk(j, m), m_r).wait_send()
        ex(j, 1, e_blk(j, m), m_l).wait_send()
        ex(j, 2, e_half(j, 0, m_l), m_r).wait_send()
        ex(j, 3, e_half(j, 1, m_r), m_l).wait_send()
        ex(j, 4, e_blk(j, m), m_s).wait_send()
        ex(j, 5, e_blk(j, m_l), m_s).wait_send()
        ex(j, 6, e_blk(j, m_r), m_s).wait_send()
        ex(j, 7, e_blk(j, m_o), m_s).wait_send()

    def g_sib(j):
        return remote(psend.at[j], precv.at[j], g_s.at[j, 0], g_r.at[j, 0], mp=m_s)

    def g_far(j, h, dev):
        return remote(q2.at[j, h], r2.at[j, h], g_s.at[j, 1 + h], g_r.at[j, 1 + h], mp=dev)

    def g_near(j, h, dev):
        return remote(q1.at[j, h], r1.at[j, h], g_s.at[j, 3 + h], g_r.at[j, 3 + h], mp=dev)

    def experts(j):
        e4(j)
        e = j % 2
        v = xbuf[e, e_rows(j), :].astype(F32)
        inv = lax.rsqrt(jnp.mean(v * v, 1, keepdims=True) + EPS)
        normed = (v * inv).astype(BF)
        g = jnp.dot(normed, wg[e], preferred_element_type=F32)
        u = jnp.dot(normed, wu[e], preferred_element_type=F32)
        abuf[...] = (g / (1.0 + jnp.exp(-g)) * u).astype(BF)
        w_far = jnp.concatenate([wd[e, :, col(i * 2 + 1 - c)] for i in range(NX)], 1)
        o_far = jnp.dot(abuf[...], w_far, preferred_element_type=F32).astype(BF)
        for i in range(NX):
            psend[j, i] = o_far[:, i * 128 : (i + 1) * 128]
        g_sib(j).start()
        w_own = jnp.concatenate([wd[e, :, col(i * 2 + c)] for i in range(NX)], 1)
        o_own = jnp.dot(abuf[...], w_own, preferred_element_type=F32)
        for i in range(NX):
            pown[j, i] = o_own[:, i * 128 : (i + 1) * 128]

    halves = (slice(0, rc // 2), slice(rc // 2, rc))

    def both(j, blk, rows=slice(None)):
        return pown[j, blk, rows] + precv[j, blk, rows].astype(F32)

    def g1(j):
        g_sib(j).wait_recv()
        q2[j, 0] = both(j, x_o, halves[0]).astype(BF)
        g_far(j, 0, m_r).start()
        q2[j, 1] = both(j, x_o, halves[1]).astype(BF)
        g_far(j, 1, m_l).start()
        q1[j, 0, halves[1]] = both(j, x_r, halves[1]).astype(BF)
        q1[j, 1, halves[0]] = both(j, x_l, halves[0]).astype(BF)

    def g2(j):
        g_far(j, 0, m_r).wait_recv()
        q1[j, 0, halves[0]] = (both(j, x_r, halves[0]) + r2[j, 0].astype(F32)).astype(BF)
        g_near(j, 0, m_r).start()
        g_far(j, 1, m_l).wait_recv()
        q1[j, 1, halves[1]] = (both(j, x_l, halves[1]) + r2[j, 1].astype(F32)).astype(BF)
        g_near(j, 1, m_l).start()

    def h_copy(p):
        k, i = divmod(p, per)
        src = hsend.at[k, :, pl.ds(i * cap, cap), :]
        if p == 0:
            return pltpu.make_async_copy(src, rbuf.at[p], h_r.at[p])
        return remote(src, rbuf.at[p], h_s.at[p], h_r.at[p], tm=tm_at(p, 1))

    def g3(j):
        g_near(j, 0, m_r).wait_recv()
        g_near(j, 1, m_l).wait_recv()
        hsend[j // 2, j % 2] = (
            both(j, x) + r1[j, 0].astype(F32) + r1[j, 1].astype(F32)
        ).astype(BF)

        for k in range(parts):

            @pl.when(j == 2 * k + 1)
            def _(k=k):
                for p in range(k * per, (k + 1) * per):
                    h_copy(p).start()

    def g_sent(j):
        g_sib(j).wait_send()
        g_far(j, 0, m_r).wait_send()
        g_far(j, 1, m_l).wait_send()
        g_near(j, 0, m_r).wait_send()
        g_near(j, 1, m_l).wait_send()

    own_g.wait()
    own_u.wait()
    own_d.wait()

    def stage(k, f):
        @pl.when((k >= 0) & (k < chunks))
        def _():
            f(k)

    @pl.loop(0, chunks + AHEAD[-1])
    def _(tick):
        for k in ORDER:
            stage(tick - AHEAD[k], (e1, e2, e3, experts, g1, g2, g3)[k])

    acc[...] = jnp.zeros_like(acc)
    for k in range(parts):
        mine = range(k * per, (k + 1) * per)
        for p in mine:
            if p == 0:
                h_copy(p).wait()
            else:
                h_copy(p).wait_recv()
        rows = slice(2 * rc * k, 2 * rc * (k + 1))
        back = rbuf[mine.start : mine.stop].reshape(2 * rc, 128)
        back_t = back.astype(F32).T.astype(BF)
        acc[...] += jnp.dot(back_t, comb_hi[rows, :], preferred_element_type=F32) + jnp.dot(
            back_t, comb_lo[rows, :], preferred_element_type=F32
        )

    out_ref[...] = (hid[...].astype(F32) + acc[...].T).astype(BF)

    halo_k.wait_send()
    halo_v.wait_send()

    @pl.loop(1, 2 * NX)
    def _(i):
        wo_copy(i).wait_send()

    @pl.loop(0, 2)
    def _(r):
        c_sent(r)

    @pl.loop(0, chunks)
    def _(j):
        e_sent(j)
        g_sent(j)

    for p in range(1, n_tm):
        d_copy(p).wait_send()
        h_copy(p).wait_send()


def per_device(
    frames_in,
    queries,
    keys,
    values,
    segment_edges,
    out_proj,
    expert_ids,
    gates,
    w_gate,
    w_up,
    w_down,
):
    frames = frames_in.shape[0]
    n_tm = lax.axis_size("tm")
    model = frames_in.shape[1]
    inner = w_gate.shape[2]
    n_exp = w_gate.shape[0] * n_tm
    cap = 4 * frames // n_exp
    parts = PARTS
    chunks = 2 * parts
    rc = n_tm // parts * cap
    slots = n_exp * cap
    vmem = pl.BlockSpec(memory_space=pltpu.VMEM)
    anyw = pl.BlockSpec(memory_space=pl.ANY)
    dma = pltpu.SemaphoreType.DMA
    return pl.pallas_call(
        functools.partial(kernel, n_tm, cap, parts),
        out_shape=jax.ShapeDtypeStruct((frames, 128), BF),
        in_specs=[vmem] * 4 + [anyw] * 7,
        out_specs=vmem,
        scratch_shapes=[
            pltpu.VMEM((LEFT + frames, 128), BF),
            pltpu.VMEM((LEFT + frames, 128), BF),
            pltpu.VMEM((frames, 128), BF),
            pltpu.VMEM((model, 128), BF),
            pltpu.VMEM(w_gate.shape, BF),
            pltpu.VMEM(w_up.shape, BF),
            pltpu.VMEM(w_down.shape, BF),
            pltpu.VMEM((frames, model), BF),
            pltpu.VMEM((frames, 128), BF),
            pltpu.VMEM((slots, frames), BF),
            pltpu.VMEM((slots, frames), BF),
            pltpu.VMEM((slots, frames), BF),
            pltpu.VMEM((n_tm, 2, cap, 128), BF),
            pltpu.VMEM((2, n_tm * cap, model), BF),
            pltpu.VMEM((rc, inner), BF),
            pltpu.VMEM((chunks, NX, rc, 128), F32),
            pltpu.VMEM((chunks, NX, rc, 128), BF),
            pltpu.VMEM((chunks, NX, rc, 128), BF),
            pltpu.VMEM((chunks, 2, rc // 2, 128), BF),
            pltpu.VMEM((chunks, 2, rc // 2, 128), BF),
            pltpu.VMEM((chunks, 2, rc, 128), BF),
            pltpu.VMEM((chunks, 2, rc, 128), BF),
            pltpu.VMEM((parts, 2, rc, 128), BF),
            pltpu.VMEM((n_tm, 2, cap, 128), BF),
            pltpu.VMEM((128, frames), F32),
            dma((7,)),
            dma((2,)),
            dma((2,)),
            dma((2 * NX,)),
            dma((2 * NX,)),
            dma((2, 8)),
            dma((2, 8)),
            dma((n_tm,)),
            dma((n_tm,)),
            dma((chunks, 8)),
            dma((chunks, 8)),
            dma((chunks, 5)),
            dma((chunks, 5)),
            dma((n_tm,)),
            dma((n_tm,)),
            pltpu.SemaphoreType.REGULAR((3,)),
        ],
        compiler_params=pltpu.CompilerParams(
            collective_id=0, has_side_effects=True, vmem_limit_bytes=56 * 1024 * 1024
        ),
        name="layer",
    )(
        segment_edges,
        expert_ids.T,
        gates.T,
        queries,
        keys,
        values,
        frames_in,
        out_proj,
        w_gate,
        w_up,
        w_down,
    )


def solution(mesh):
    return jax.shard_map(
        per_device,
        mesh=mesh,
        in_specs=(
            P("tm", None),
            P("tm", "mp"),
            P("tm", "mp"),
            P("tm", "mp"),
            P(None, "tm"),
            P("mp", None),
            P("tm", None),
            P("tm", None),
            P("tm", None, "mp"),
            P("tm", None, "mp"),
            P("tm", "mp", None),
        ),
        out_specs=P("tm", "mp"),
        check_vma=False,
    )
```

```python
import functools

import jax
import jax.numpy as jnp
from jax import lax
from jax.experimental import pallas as pl
from jax.experimental.pallas import tpu as pltpu
from jax.sharding import PartitionSpec as P

HEADS = 16
LEFT = 256
EPS = 1e-06
NX = 4
NY = 4
QB = 128
PARTS = 4
AHEAD = (0, 2, 4, 5, 7, 9, 11)
ORDER = (0, 6, 5, 4, 1, 2, 3)
MESH = pl.DeviceIdType.MESH
NEG = -1e30
BF = jnp.bfloat16
F32 = jnp.float32


def relative_order(nz, parts):
    cells = sorted(
        ((dy, dz) for dy in range(NY) for dz in range(nz)),
        key=lambda o: min(o[0], NY - o[0]) + min(o[1], nz - o[1]),
    )
    size = len(cells) // parts
    groups = [cells[i * size : (i + 1) * size] for i in range(parts)]
    return sum(groups[::2] + groups[1::2][::-1], [])


def kernel(
    n_tm,
    cap,
    parts,
    edges_ref,
    ids_ref,
    gates_ref,
    q_ref,
    k_hbm,
    v_hbm,
    f_hbm,
    wo_hbm,
    wg_hbm,
    wu_hbm,
    wd_hbm,
    out_ref,
    kbuf,
    vbuf,
    fbuf,
    wo,
    wg,
    wu,
    wd,
    ctx,
    hid,
    onehot,
    comb_hi,
    comb_lo,
    sbuf,
    xbuf,
    abuf,
    pown,
    psend,
    precv,
    q2,
    r2,
    q1,
    r1,
    hsend,
    rbuf,
    acc,
    loc_sem,
    halo_s,
    halo_r,
    wo_s,
    wo_r,
    c_s,
    c_r,
    d_s,
    d_r,
    e_s,
    e_r,
    g_s,
    g_r,
    h_s,
    h_r,
    know,
):
    t = lax.axis_index("tm")
    m = lax.axis_index("mp")
    nz = n_tm // NY
    y, z = t // nz, t % nz
    x, c = m // 2, m % 2
    x_r, x_l, x_o = (x + 1) % NX, (x + NX - 1) % NX, (x + 2) % NX
    m_r, m_l, m_o, m_s = x_r * 2 + c, x_l * 2 + c, x_o * 2 + c, x * 2 + 1 - c
    frames = q_ref.shape[0]
    n_exp = 2 * n_tm
    per = n_tm // parts
    rc = per * cap
    chunks = 2 * parts
    offsets = relative_order(nz, parts)
    nxt, prv = (t + 1) % n_tm, (t + n_tm - 1) % n_tm

    def col(i):
        return pl.ds(pl.multiple_of(i * 128, 128), 128)

    def remote(src, dst, ss, rs, **dev):
        return pltpu.make_async_remote_copy(
            src_ref=src, dst_ref=dst, send_sem=ss, recv_sem=rs, device_id=dev, device_id_type=MESH
        )

    barrier = pltpu.get_barrier_semaphore()

    def tell(sem, dy, dz):
        pl.semaphore_signal(
            sem, inc=1, device_id={"tm": (y + dy) % NY * nz + (z + dz) % nz}, device_id_type=MESH
        )

    for dy in range(1, NY):
        tell(barrier, dy, 0)
    if nz > 1:
        tell(barrier, 0, 1)
        tell(barrier, 0, nz - 1)
    for peer in (nxt, prv):
        pl.semaphore_signal(barrier, inc=1, device_id={"tm": peer}, device_id_type=MESH)

    @pl.loop(1, 2 * NX)
    def _(i):
        pl.semaphore_signal(barrier, inc=1, device_id={"mp": (m + i) % (2 * NX)}, device_id_type=MESH)

    own_k = pltpu.make_async_copy(k_hbm, kbuf.at[pl.ds(LEFT, frames)], loc_sem.at[0])
    own_v = pltpu.make_async_copy(v_hbm, vbuf.at[pl.ds(LEFT, frames)], loc_sem.at[1])
    own_f = pltpu.make_async_copy(f_hbm.at[:, col(m)], fbuf, loc_sem.at[2])
    own_o = pltpu.make_async_copy(
        wo_hbm.at[:, col(m)], wo.at[pl.ds(pl.multiple_of(m * 128, 128), 128)], loc_sem.at[3]
    )
    own_g = pltpu.make_async_copy(wg_hbm, wg, loc_sem.at[4])
    own_u = pltpu.make_async_copy(wu_hbm, wu, loc_sem.at[5])
    own_d = pltpu.make_async_copy(wd_hbm, wd, loc_sem.at[6])
    for copy in (own_k, own_v, own_f, own_o, own_g, own_u, own_d):
        copy.start()

    halo_k = remote(
        k_hbm.at[pl.ds(frames - LEFT, LEFT)], kbuf.at[pl.ds(0, LEFT)], halo_s.at[0], halo_r.at[0], tm=nxt
    )
    halo_v = remote(
        v_hbm.at[pl.ds(frames - LEFT, LEFT)], vbuf.at[pl.ds(0, LEFT)], halo_s.at[1], halo_r.at[1], tm=nxt
    )

    def wo_copy(i):
        peer = (m + i) % (2 * NX)
        return remote(
            wo_hbm.at[:, col(peer)],
            wo.at[pl.ds(pl.multiple_of(m * 128, 128), 128)],
            wo_s.at[i],
            wo_r.at[i],
            mp=peer,
        )

    scale = (wo_hbm.shape[1] // HEADS) ** (-0.5)
    head = wo_hbm.shape[1] // HEADS
    lane = lax.broadcasted_iota(jnp.int32, (QB, 128), 1)
    win = LEFT + QB

    def attend(b):
        rows = pl.ds(pl.multiple_of(b * QB, QB), QB)
        keys = pl.ds(pl.multiple_of(b * QB, QB), win)
        q = q_ref[rows, :].astype(F32) * scale
        q_both = jnp.concatenate(
            [jnp.where(lane < head, q, 0.0), jnp.where(lane >= head, q, 0.0)], 0
        ).astype(BF)
        s = lax.dot_general(
            kbuf[keys, :], q_both, (((1,), (1,)), ((), ())), preferred_element_type=F32
        )
        lower = jnp.maximum(edges_ref[0:1, rows] - LEFT, 0)
        upper = edges_ref[1:2, rows]
        lower = jnp.concatenate([lower, lower], 1)
        upper = jnp.concatenate([upper, upper], 1)
        place = lax.broadcasted_iota(jnp.int32, (win, 2 * QB), 0) + (t * frames - LEFT + b * QB)
        s = jnp.where((place >= lower) & (place <= upper), s, NEG)
        p = jnp.exp(s - jnp.max(s, 0, keepdims=True))
        total = jnp.sum(p, 0, keepdims=True)
        v_t = vbuf[keys, :].astype(F32).T.astype(BF)
        o = jnp.dot(v_t, p.astype(BF), preferred_element_type=F32) / total
        both = jnp.concatenate([o[:head, :QB], o[head:, QB:]], 0)
        ctx[m, rows] = both.T.astype(BF)

    half = frames // 2

    def c_rows(r):
        return pl.ds(pl.multiple_of(r * half, half), half)

    def cx(r, k, rows, blk, dev):
        ref = ctx.at[blk, rows]
        return remote(ref, ref, c_s.at[r, k], c_r.at[r, k], mp=dev)

    def c1(r):
        cx(r, 0, c_rows(r), m, m_r).start()
        cx(r, 1, c_rows(r), m, m_l).start()
        cx(r, 2, c_rows(r), m, m_o).start()
        cx(r, 3, c_rows(r), m, m_s).start()

    def other(i):
        return i + 1 - 2 * c

    def c2(r):
        cx(r, 0, c_rows(r), m_l, m_r).wait_recv()
        cx(r, 4, c_rows(r), m_l, m_s).start()
        cx(r, 1, c_rows(r), m_r, m_l).wait_recv()
        cx(r, 5, c_rows(r), m_r, m_s).start()
        cx(r, 2, c_rows(r), m_o, m_o).wait_recv()
        cx(r, 6, c_rows(r), m_o, m_s).start()

    def c3(r):
        cx(r, 3, c_rows(r), other(m), m_s).wait_recv()
        cx(r, 4, c_rows(r), other(m_l), m_s).wait_recv()
        cx(r, 5, c_rows(r), other(m_r), m_s).wait_recv()
        cx(r, 6, c_rows(r), other(m_o), m_s).wait_recv()

    def c_sent(r):
        cx(r, 0, c_rows(r), m, m_r).wait_send()
        cx(r, 1, c_rows(r), m, m_l).wait_send()
        cx(r, 2, c_rows(r), m, m_o).wait_send()
        cx(r, 3, c_rows(r), m, m_s).wait_send()
        cx(r, 4, c_rows(r), m_l, m_s).wait_send()
        cx(r, 5, c_rows(r), m_r, m_s).wait_send()
        cx(r, 6, c_rows(r), m_o, m_s).wait_send()

    own_k.wait()
    own_v.wait()
    per_half = half // QB

    @pl.loop(per_half, 2 * per_half)
    def _(b):
        attend(b)

    pl.semaphore_wait(barrier, NY - 1 + 2 * (nz > 1) + 2 + 2 * NX - 1)
    halo_k.start()
    halo_v.start()
    c1(1)

    @pl.loop(1, 2 * NX)
    def _(i):
        wo_copy(i).start()

    if nz > 1:
        tell(know.at[0], 0, 1)
        tell(know.at[0], 0, nz - 1)

    id0, id1 = ids_ref[0:1, :], ids_ref[1:2, :]
    e_iota = lax.broadcasted_iota(jnp.int32, (n_exp, frames), 0)
    is0, is1 = e_iota == id0, e_iota == id1
    named = jnp.where(is0 | is1, 1.0, 0.0).astype(BF)
    before = jnp.where(
        lax.broadcasted_iota(jnp.int32, (frames, frames), 0)
        < lax.broadcasted_iota(jnp.int32, (frames, frames), 1),
        1.0,
        0.0,
    ).astype(BF)
    ranks = jnp.dot(named, before, preferred_element_type=F32)
    slot0 = jnp.sum(jnp.where(is0, ranks, 0.0), 0, keepdims=True).astype(jnp.int32)
    slot1 = jnp.sum(jnp.where(is1, ranks, 0.0), 0, keepdims=True).astype(jnp.int32)
    owner = lax.broadcasted_iota(jnp.int32, (n_exp, frames), 0)
    first = jnp.zeros((n_exp, frames), jnp.int32)
    for p, (dy, dz) in enumerate(offsets):
        d = (y + NY - dy) % NY * nz + (z + nz - dz) % nz
        first = jnp.where((owner == 2 * d) | (owner == 2 * d + 1), (2 * p - 2 * d) * cap, first)
    first = first + owner * cap
    tgt0 = slot0 + jnp.sum(jnp.where(is0, first, 0), 0, keepdims=True)
    tgt1 = slot1 + jnp.sum(jnp.where(is1, first, 0), 0, keepdims=True)

    @pl.loop(0, n_exp * cap // 128)
    def _(i):
        rows = pl.ds(pl.multiple_of(i * 128, 128), 128)
        place = lax.broadcasted_iota(jnp.int32, (128, frames), 0) + i * 128
        onehot[rows, :] = jnp.where((place == tgt0) | (place == tgt1), 1.0, 0.0).astype(BF)

    if nz > 1:
        pl.semaphore_wait(know.at[0], 2)
        tell(know.at[1], 0, 2 % nz)
        tell(know.at[1], 0, nz - 2)
    c2(1)
    halo_k.wait_recv()
    halo_v.wait_recv()

    @pl.loop(0, per_half)
    def _(b):
        attend(b)

    c1(0)
    c3(1)
    if nz > 1:
        pl.semaphore_wait(know.at[1], 2)
    for dy in range(1, NY):
        tell(know.at[2], dy, 0)

    g0, g1 = gates_ref[0:1, :], gates_ref[1:2, :]
    g0_hi, g1_hi = g0.astype(BF).astype(F32), g1.astype(BF).astype(F32)
    g0_lo, g1_lo = g0 - g0_hi, g1 - g1_hi

    @pl.loop(0, n_exp * cap // 128)
    def _(i):
        rows = pl.ds(pl.multiple_of(i * 128, 128), 128)
        place = lax.broadcasted_iota(jnp.int32, (128, frames), 0) + i * 128
        at0, at1 = place == tgt0, place == tgt1
        comb_hi[rows, :] = jnp.where(at0, g0_hi, jnp.where(at1, g1_hi, 0.0)).astype(BF)
        comb_lo[rows, :] = jnp.where(at0, g0_lo, jnp.where(at1, g1_lo, 0.0)).astype(BF)

    @pl.loop(1, 2 * NX)
    def _(i):
        wo_copy(i).wait_recv()

    own_o.wait()
    own_f.wait()

    def hidden(r):
        rows = c_rows(r)
        mixed = jnp.concatenate([ctx[b, rows] for b in range(2 * NX)], 1)
        hid[rows, :] = (
            fbuf[rows, :].astype(F32) + jnp.dot(mixed, wo[...], preferred_element_type=F32)
        ).astype(BF)

    hidden(1)
    c2(0)
    c3(0)
    hidden(0)
    pl.semaphore_wait(know.at[2], NY - 1)

    def spot(i):
        return i % 2 * NX + i // 2 % 2 * 2 + i // 4

    def tm_at(p, sign):
        dy, dz = offsets[p]
        return (y + NY + sign * dy) % NY * nz + (z + nz + sign * dz) % nz

    def x_rows(p):
        return pl.ds(p * cap, cap)

    def d_copy(p):
        if p == 0:
            return pltpu.make_async_copy(sbuf.at[p], xbuf.at[spot(m), :, x_rows(p)], d_r.at[p])
        return remote(
            sbuf.at[p], xbuf.at[spot(m), :, x_rows(p)], d_s.at[p], d_r.at[p], tm=tm_at(p, -1)
        )

    def d_wait(p):
        if p == 0:
            d_copy(p).wait()
        else:
            d_copy(p).wait_recv()

    sent_rows = n_tm * 2 * cap // 4
    for i in range(4):
        sent = jnp.dot(
            onehot[i * sent_rows : (i + 1) * sent_rows, :], hid[...], preferred_element_type=F32
        )
        sbuf[i * n_tm // 4 : (i + 1) * n_tm // 4] = sent.astype(BF).reshape(n_tm // 4, 2, cap, 128)
        for p in range(i * n_tm // 4, (i + 1) * n_tm // 4):
            d_copy(p).start()

    def e_rows(j):
        return pl.ds(pl.multiple_of(j // 2 * rc, rc), rc)

    def ex(j, k, ref, dev):
        return remote(ref, ref, e_s.at[j, k], e_r.at[j, k], mp=dev)

    def e_blk(j, blk):
        return xbuf.at[spot(blk), j % 2, e_rows(j)]

    def e_half(j, h, blk):
        rows = pl.ds(pl.multiple_of(j // 2 * rc + h * (rc // 2), rc // 2), rc // 2)
        return xbuf.at[spot(blk), j % 2, rows]

    def e_pair(j, core, odd):
        return xbuf.at[pl.ds(core * NX + odd * 2, 2), j % 2, e_rows(j)]

    near, same = (x + 1) % 2, x % 2

    def e1(j):
        for k in range(parts):

            @pl.when(j == 2 * k)
            def _(k=k):
                for p in range(k * per, (k + 1) * per):
                    d_wait(p)

        ex(j, 0, e_blk(j, m), m_r).start()
        ex(j, 1, e_blk(j, m), m_l).start()

    def e2(j):
        ex(j, 0, e_blk(j, m_l), m_r).wait_recv()
        ex(j, 2, e_half(j, 0, m_l), m_r).start()
        ex(j, 1, e_blk(j, m_r), m_l).wait_recv()
        ex(j, 3, e_half(j, 1, m_r), m_l).start()
        ex(j, 4, e_pair(j, c, near), m_s).start()

    def e3(j):
        ex(j, 2, e_half(j, 0, m_o), m_r).wait_recv()
        ex(j, 3, e_half(j, 1, m_o), m_l).wait_recv()
        ex(j, 5, e_pair(j, c, same), m_s).start()

    def e4(j):
        ex(j, 4, e_pair(j, 1 - c, near), m_s).wait_recv()
        ex(j, 5, e_pair(j, 1 - c, same), m_s).wait_recv()

    def e_sent(j):
        ex(j, 0, e_blk(j, m), m_r).wait_send()
        ex(j, 1, e_blk(j, m), m_l).wait_send()
        ex(j, 2, e_half(j, 0, m_l), m_r).wait_send()
        ex(j, 3, e_half(j, 1, m_r), m_l).wait_send()
        ex(j, 4, e_pair(j, c, near), m_s).wait_send()
        ex(j, 5, e_pair(j, c, same), m_s).wait_send()

    def g_sib(j):
        return remote(psend.at[j], precv.at[j], g_s.at[j, 0], g_r.at[j, 0], mp=m_s)

    def g_far(j, h, dev):
        return remote(q2.at[j, h], r2.at[j, h], g_s.at[j, 1 + h], g_r.at[j, 1 + h], mp=dev)

    def g_near(j, h, dev):
        return remote(q1.at[j, h], r1.at[j, h], g_s.at[j, 3 + h], g_r.at[j, 3 + h], mp=dev)

    def experts(j):
        e4(j)
        e = j % 2
        v = jnp.concatenate([xbuf[spot(b), e, e_rows(j)] for b in range(2 * NX)], 1).astype(F32)
        inv = lax.rsqrt(jnp.mean(v * v, 1, keepdims=True) + EPS)
        normed = (v * inv).astype(BF)
        g = jnp.dot(normed, wg[e], preferred_element_type=F32)
        u = jnp.dot(normed, wu[e], preferred_element_type=F32)
        abuf[...] = (g / (1.0 + jnp.exp(-g)) * u).astype(BF)
        w_far = jnp.concatenate([wd[e, :, col(i * 2 + 1 - c)] for i in range(NX)], 1)
        o_far = jnp.dot(abuf[...], w_far, preferred_element_type=F32).astype(BF)
        for i in range(NX):
            psend[j, i] = o_far[:, i * 128 : (i + 1) * 128]
        g_sib(j).start()
        w_own = jnp.concatenate([wd[e, :, col(i * 2 + c)] for i in range(NX)], 1)
        o_own = jnp.dot(abuf[...], w_own, preferred_element_type=F32)
        for i in range(NX):
            pown[j, i] = o_own[:, i * 128 : (i + 1) * 128]

    halves = (slice(0, rc // 2), slice(rc // 2, rc))

    def both(j, blk, rows=slice(None)):
        return pown[j, blk, rows] + precv[j, blk, rows].astype(F32)

    def g1(j):
        g_sib(j).wait_recv()
        q2[j, 0] = both(j, x_o, halves[0]).astype(BF)
        g_far(j, 0, m_r).start()
        q2[j, 1] = both(j, x_o, halves[1]).astype(BF)
        g_far(j, 1, m_l).start()
        q1[j, 0, halves[1]] = both(j, x_r, halves[1]).astype(BF)
        q1[j, 1, halves[0]] = both(j, x_l, halves[0]).astype(BF)

    def g2(j):
        g_far(j, 0, m_r).wait_recv()
        q1[j, 0, halves[0]] = (both(j, x_r, halves[0]) + r2[j, 0].astype(F32)).astype(BF)
        g_near(j, 0, m_r).start()
        g_far(j, 1, m_l).wait_recv()
        q1[j, 1, halves[1]] = (both(j, x_l, halves[1]) + r2[j, 1].astype(F32)).astype(BF)
        g_near(j, 1, m_l).start()

    def h_copy(p):
        k, i = divmod(p, per)
        src = hsend.at[k, :, pl.ds(i * cap, cap), :]
        if p == 0:
            return pltpu.make_async_copy(src, rbuf.at[p], h_r.at[p])
        return remote(src, rbuf.at[p], h_s.at[p], h_r.at[p], tm=tm_at(p, 1))

    def g3(j):
        g_near(j, 0, m_r).wait_recv()
        g_near(j, 1, m_l).wait_recv()
        hsend[j // 2, j % 2] = (
            both(j, x) + r1[j, 0].astype(F32) + r1[j, 1].astype(F32)
        ).astype(BF)

        for k in range(parts):

            @pl.when(j == 2 * k + 1)
            def _(k=k):
                for p in range(k * per, (k + 1) * per):
                    h_copy(p).start()

    def g_sent(j):
        g_sib(j).wait_send()
        g_far(j, 0, m_r).wait_send()
        g_far(j, 1, m_l).wait_send()
        g_near(j, 0, m_r).wait_send()
        g_near(j, 1, m_l).wait_send()

    own_g.wait()
    own_u.wait()
    own_d.wait()

    def stage(k, f):
        @pl.when((k >= 0) & (k < chunks))
        def _():
            f(k)

    @pl.loop(0, chunks + AHEAD[-1])
    def _(tick):
        for k in ORDER:
            stage(tick - AHEAD[k], (e1, e2, e3, experts, g1, g2, g3)[k])

    def sent():
        halo_k.wait_send()
        halo_v.wait_send()

        @pl.loop(1, 2 * NX)
        def _(i):
            wo_copy(i).wait_send()

        @pl.loop(0, 2)
        def _(r):
            c_sent(r)

        @pl.loop(0, chunks)
        def _(j):
            e_sent(j)
            g_sent(j)

        for p in range(1, n_tm):
            d_copy(p).wait_send()
        for p in range(1, (parts - 1) * per):
            h_copy(p).wait_send()

    acc[...] = jnp.zeros_like(acc)
    for k in range(parts):
        if k == parts - 1:
            sent()
        mine = range(k * per, (k + 1) * per)
        for p in mine:
            if p == 0:
                h_copy(p).wait()
            else:
                h_copy(p).wait_recv()
        rows = slice(2 * rc * k, 2 * rc * (k + 1))
        back = rbuf[mine.start : mine.stop].reshape(2 * rc, 128)
        back_t = back.astype(F32).T.astype(BF)
        acc[...] += jnp.dot(back_t, comb_hi[rows, :], preferred_element_type=F32) + jnp.dot(
            back_t, comb_lo[rows, :], preferred_element_type=F32
        )

    out_ref[...] = (hid[...].astype(F32) + acc[...].T).astype(BF)

    for p in range((parts - 1) * per, n_tm):
        if p > 0:
            h_copy(p).wait_send()


def per_device(
    frames_in,
    queries,
    keys,
    values,
    segment_edges,
    out_proj,
    expert_ids,
    gates,
    w_gate,
    w_up,
    w_down,
):
    frames = frames_in.shape[0]
    n_tm = lax.axis_size("tm")
    model = frames_in.shape[1]
    inner = w_gate.shape[2]
    n_exp = w_gate.shape[0] * n_tm
    cap = 4 * frames // n_exp
    parts = PARTS
    chunks = 2 * parts
    rc = n_tm // parts * cap
    slots = n_exp * cap
    vmem = pl.BlockSpec(memory_space=pltpu.VMEM)
    anyw = pl.BlockSpec(memory_space=pl.ANY)
    dma = pltpu.SemaphoreType.DMA
    return pl.pallas_call(
        functools.partial(kernel, n_tm, cap, parts),
        out_shape=jax.ShapeDtypeStruct((frames, 128), BF),
        in_specs=[vmem] * 4 + [anyw] * 7,
        out_specs=vmem,
        scratch_shapes=[
            pltpu.VMEM((LEFT + frames, 128), BF),
            pltpu.VMEM((LEFT + frames, 128), BF),
            pltpu.VMEM((frames, 128), BF),
            pltpu.VMEM((model, 128), BF),
            pltpu.VMEM(w_gate.shape, BF),
            pltpu.VMEM(w_up.shape, BF),
            pltpu.VMEM(w_down.shape, BF),
            pltpu.VMEM((model // 128, frames, 128), BF),
            pltpu.VMEM((frames, 128), BF),
            pltpu.VMEM((slots, frames), BF),
            pltpu.VMEM((slots, frames), BF),
            pltpu.VMEM((slots, frames), BF),
            pltpu.VMEM((n_tm, 2, cap, 128), BF),
            pltpu.VMEM((model // 128, 2, n_tm * cap, 128), BF),
            pltpu.VMEM((rc, inner), BF),
            pltpu.VMEM((chunks, NX, rc, 128), F32),
            pltpu.VMEM((chunks, NX, rc, 128), BF),
            pltpu.VMEM((chunks, NX, rc, 128), BF),
            pltpu.VMEM((chunks, 2, rc // 2, 128), BF),
            pltpu.VMEM((chunks, 2, rc // 2, 128), BF),
            pltpu.VMEM((chunks, 2, rc, 128), BF),
            pltpu.VMEM((chunks, 2, rc, 128), BF),
            pltpu.VMEM((parts, 2, rc, 128), BF),
            pltpu.VMEM((n_tm, 2, cap, 128), BF),
            pltpu.VMEM((128, frames), F32),
            dma((7,)),
            dma((2,)),
            dma((2,)),
            dma((2 * NX,)),
            dma((2 * NX,)),
            dma((2, 8)),
            dma((2, 8)),
            dma((n_tm,)),
            dma((n_tm,)),
            dma((chunks, 6)),
            dma((chunks, 6)),
            dma((chunks, 5)),
            dma((chunks, 5)),
            dma((n_tm,)),
            dma((n_tm,)),
            pltpu.SemaphoreType.REGULAR((3,)),
        ],
        compiler_params=pltpu.CompilerParams(
            collective_id=0, has_side_effects=True, vmem_limit_bytes=56 * 1024 * 1024
        ),
        name="layer",
    )(
        segment_edges,
        expert_ids.T,
        gates.T,
        queries,
        keys,
        values,
        frames_in,
        out_proj,
        w_gate,
        w_up,
        w_down,
    )


def solution(mesh):
    return jax.shard_map(
        per_device,
        mesh=mesh,
        in_specs=(
            P("tm", None),
            P("tm", "mp"),
            P("tm", "mp"),
            P("tm", "mp"),
            P(None, "tm"),
            P("mp", None),
            P("tm", None),
            P("tm", None),
            P("tm", None, "mp"),
            P("tm", None, "mp"),
            P("tm", "mp", None),
        ),
        out_specs=P("tm", "mp"),
        check_vma=False,
    )
```

```python
import functools

import jax
import jax.numpy as jnp
from jax import lax
from jax.experimental import pallas as pl
from jax.experimental.pallas import tpu as pltpu
from jax.sharding import PartitionSpec as P

HEADS = 16
LEFT = 256
EPS = 1e-06
NX = 4
NY = 4
QB = 128
PARTS = 4
AHEAD = (0, 2, 4, 5, 7, 9, 11)
ORDER = (0, 6, 5, 4, 1, 2, 3)
MESH = pl.DeviceIdType.MESH
NEG = -1e30
BF = jnp.bfloat16
F32 = jnp.float32


def relative_order(nz, parts):
    cells = sorted(
        ((dy, dz) for dy in range(NY) for dz in range(nz)),
        key=lambda o: min(o[0], NY - o[0]) + min(o[1], nz - o[1]),
    )
    size = len(cells) // parts
    groups = [cells[i * size : (i + 1) * size] for i in range(parts)]
    return sum(groups[::2] + groups[1::2][::-1], [])


def kernel(
    n_tm,
    cap,
    parts,
    edges_ref,
    ids_ref,
    gates_ref,
    q_ref,
    k_hbm,
    v_hbm,
    f_hbm,
    wo_hbm,
    wg_hbm,
    wu_hbm,
    wd_hbm,
    out_ref,
    kbuf,
    vbuf,
    fbuf,
    wo,
    wg,
    wu,
    wd,
    ctx,
    hid,
    onehot,
    comb_hi,
    comb_lo,
    sbuf,
    xbuf,
    abuf,
    pown,
    psend,
    precv,
    q2,
    r2,
    q1,
    r1,
    hsend,
    rbuf,
    acc,
    loc_sem,
    halo_s,
    halo_r,
    wo_s,
    wo_r,
    c_s,
    c_r,
    d_s,
    d_r,
    e_s,
    e_r,
    g_s,
    g_r,
    h_s,
    h_r,
    know,
):
    t = lax.axis_index("tm")
    m = lax.axis_index("mp")
    nz = n_tm // NY
    y, z = t // nz, t % nz
    x, c = m // 2, m % 2
    x_r, x_l, x_o = (x + 1) % NX, (x + NX - 1) % NX, (x + 2) % NX
    m_r, m_l, m_o, m_s = x_r * 2 + c, x_l * 2 + c, x_o * 2 + c, x * 2 + 1 - c
    frames = q_ref.shape[0]
    n_exp = 2 * n_tm
    per = n_tm // parts
    rc = per * cap
    chunks = 2 * parts
    offsets = relative_order(nz, parts)
    nxt, prv = (t + 1) % n_tm, (t + n_tm - 1) % n_tm

    def col(i):
        return pl.ds(pl.multiple_of(i * 128, 128), 128)

    def remote(src, dst, ss, rs, **dev):
        return pltpu.make_async_remote_copy(
            src_ref=src, dst_ref=dst, send_sem=ss, recv_sem=rs, device_id=dev, device_id_type=MESH
        )

    barrier = pltpu.get_barrier_semaphore()

    def tell(sem, dy, dz):
        pl.semaphore_signal(
            sem, inc=1, device_id={"tm": (y + dy) % NY * nz + (z + dz) % nz}, device_id_type=MESH
        )

    for dy in range(1, NY):
        tell(barrier, dy, 0)
    if nz > 1:
        tell(barrier, 0, 1)
        tell(barrier, 0, nz - 1)
    for peer in (nxt, prv):
        pl.semaphore_signal(barrier, inc=1, device_id={"tm": peer}, device_id_type=MESH)

    @pl.loop(1, 2 * NX)
    def _(i):
        pl.semaphore_signal(barrier, inc=1, device_id={"mp": (m + i) % (2 * NX)}, device_id_type=MESH)

    own_k = pltpu.make_async_copy(k_hbm, kbuf.at[pl.ds(LEFT, frames)], loc_sem.at[0])
    own_v = pltpu.make_async_copy(v_hbm, vbuf.at[pl.ds(LEFT, frames)], loc_sem.at[1])
    own_f = pltpu.make_async_copy(f_hbm.at[:, col(m)], fbuf, loc_sem.at[2])
    own_o = pltpu.make_async_copy(
        wo_hbm.at[:, col(m)], wo.at[pl.ds(pl.multiple_of(m * 128, 128), 128)], loc_sem.at[3]
    )
    own_g = pltpu.make_async_copy(wg_hbm, wg, loc_sem.at[4])
    own_u = pltpu.make_async_copy(wu_hbm, wu, loc_sem.at[5])
    own_d = pltpu.make_async_copy(wd_hbm, wd, loc_sem.at[6])
    for copy in (own_k, own_v, own_f, own_o, own_g, own_u, own_d):
        copy.start()

    halo_k = remote(
        k_hbm.at[pl.ds(frames - LEFT, LEFT)], kbuf.at[pl.ds(0, LEFT)], halo_s.at[0], halo_r.at[0], tm=nxt
    )
    halo_v = remote(
        v_hbm.at[pl.ds(frames - LEFT, LEFT)], vbuf.at[pl.ds(0, LEFT)], halo_s.at[1], halo_r.at[1], tm=nxt
    )

    def wo_copy(i):
        peer = (m + i) % (2 * NX)
        return remote(
            wo_hbm.at[:, col(peer)],
            wo.at[pl.ds(pl.multiple_of(m * 128, 128), 128)],
            wo_s.at[i],
            wo_r.at[i],
            mp=peer,
        )

    scale = (wo_hbm.shape[1] // HEADS) ** (-0.5)
    head = wo_hbm.shape[1] // HEADS
    lane = lax.broadcasted_iota(jnp.int32, (QB, 128), 1)
    win = LEFT + QB

    def attend(b):
        rows = pl.ds(pl.multiple_of(b * QB, QB), QB)
        keys = pl.ds(pl.multiple_of(b * QB, QB), win)
        q = q_ref[rows, :].astype(F32) * scale
        q_both = jnp.concatenate(
            [jnp.where(lane < head, q, 0.0), jnp.where(lane >= head, q, 0.0)], 0
        ).astype(BF)
        s = lax.dot_general(
            kbuf[keys, :], q_both, (((1,), (1,)), ((), ())), preferred_element_type=F32
        )
        lower = jnp.maximum(edges_ref[0:1, rows] - LEFT, 0)
        upper = edges_ref[1:2, rows]
        lower = jnp.concatenate([lower, lower], 1)
        upper = jnp.concatenate([upper, upper], 1)
        place = lax.broadcasted_iota(jnp.int32, (win, 2 * QB), 0) + (t * frames - LEFT + b * QB)
        s = jnp.where((place >= lower) & (place <= upper), s, NEG)
        p = jnp.exp(s - jnp.max(s, 0, keepdims=True))
        total = jnp.sum(p, 0, keepdims=True)
        v_t = vbuf[keys, :].astype(F32).T.astype(BF)
        o = jnp.dot(v_t, p.astype(BF), preferred_element_type=F32) / total
        both = jnp.concatenate([o[:head, :QB], o[head:, QB:]], 0)
        ctx[m, rows] = both.T.astype(BF)

    half = frames // 2

    def c_rows(r):
        return pl.ds(pl.multiple_of(r * half, half), half)

    def cx(r, k, rows, blk, dev):
        ref = ctx.at[blk, rows]
        return remote(ref, ref, c_s.at[r, k], c_r.at[r, k], mp=dev)

    def c1(r):
        cx(r, 0, c_rows(r), m, m_r).start()
        cx(r, 1, c_rows(r), m, m_l).start()
        cx(r, 2, c_rows(r), m, m_o).start()
        cx(r, 3, c_rows(r), m, m_s).start()

    def other(i):
        return i + 1 - 2 * c

    def c2(r):
        cx(r, 0, c_rows(r), m_l, m_r).wait_recv()
        cx(r, 4, c_rows(r), m_l, m_s).start()
        cx(r, 1, c_rows(r), m_r, m_l).wait_recv()
        cx(r, 5, c_rows(r), m_r, m_s).start()
        cx(r, 2, c_rows(r), m_o, m_o).wait_recv()
        cx(r, 6, c_rows(r), m_o, m_s).start()

    def c3(r):
        cx(r, 3, c_rows(r), other(m), m_s).wait_recv()
        cx(r, 4, c_rows(r), other(m_l), m_s).wait_recv()
        cx(r, 5, c_rows(r), other(m_r), m_s).wait_recv()
        cx(r, 6, c_rows(r), other(m_o), m_s).wait_recv()

    def c_sent(r):
        cx(r, 0, c_rows(r), m, m_r).wait_send()
        cx(r, 1, c_rows(r), m, m_l).wait_send()
        cx(r, 2, c_rows(r), m, m_o).wait_send()
        cx(r, 3, c_rows(r), m, m_s).wait_send()
        cx(r, 4, c_rows(r), m_l, m_s).wait_send()
        cx(r, 5, c_rows(r), m_r, m_s).wait_send()
        cx(r, 6, c_rows(r), m_o, m_s).wait_send()

    pl.semaphore_wait(barrier, NY - 1 + 2 * (nz > 1) + 2 + 2 * NX - 1)
    halo_k.start()
    halo_v.start()
    own_k.wait()
    own_v.wait()
    per_half = half // QB

    @pl.loop(per_half, 2 * per_half)
    def _(b):
        attend(b)

    c1(1)

    @pl.loop(1, 2 * NX)
    def _(i):
        wo_copy(i).start()

    if nz > 1:
        tell(know.at[0], 0, 1)
        tell(know.at[0], 0, nz - 1)

    id0, id1 = ids_ref[0:1, :], ids_ref[1:2, :]
    e_iota = lax.broadcasted_iota(jnp.int32, (n_exp, frames), 0)
    is0, is1 = e_iota == id0, e_iota == id1
    named = jnp.where(is0 | is1, 1.0, 0.0).astype(BF)
    before = jnp.where(
        lax.broadcasted_iota(jnp.int32, (frames, frames), 0)
        < lax.broadcasted_iota(jnp.int32, (frames, frames), 1),
        1.0,
        0.0,
    ).astype(BF)
    ranks = jnp.dot(named, before, preferred_element_type=F32)
    slot0 = jnp.sum(jnp.where(is0, ranks, 0.0), 0, keepdims=True).astype(jnp.int32)
    slot1 = jnp.sum(jnp.where(is1, ranks, 0.0), 0, keepdims=True).astype(jnp.int32)
    owner = lax.broadcasted_iota(jnp.int32, (n_exp, frames), 0)
    first = jnp.zeros((n_exp, frames), jnp.int32)
    for p, (dy, dz) in enumerate(offsets):
        d = (y + NY - dy) % NY * nz + (z + nz - dz) % nz
        first = jnp.where((owner == 2 * d) | (owner == 2 * d + 1), (2 * p - 2 * d) * cap, first)
    first = first + owner * cap
    tgt0 = slot0 + jnp.sum(jnp.where(is0, first, 0), 0, keepdims=True)
    tgt1 = slot1 + jnp.sum(jnp.where(is1, first, 0), 0, keepdims=True)

    @pl.loop(0, n_exp * cap // 128)
    def _(i):
        rows = pl.ds(pl.multiple_of(i * 128, 128), 128)
        place = lax.broadcasted_iota(jnp.int32, (128, frames), 0) + i * 128
        onehot[rows, :] = jnp.where((place == tgt0) | (place == tgt1), 1.0, 0.0).astype(BF)

    if nz > 1:
        pl.semaphore_wait(know.at[0], 2)
        tell(know.at[1], 0, 2 % nz)
        tell(know.at[1], 0, nz - 2)
    c2(1)
    halo_k.wait_recv()
    halo_v.wait_recv()

    @pl.loop(0, per_half)
    def _(b):
        attend(b)

    c1(0)
    c3(1)
    if nz > 1:
        pl.semaphore_wait(know.at[1], 2)
    for dy in range(1, NY):
        tell(know.at[2], dy, 0)

    g0, g1 = gates_ref[0:1, :], gates_ref[1:2, :]
    g0_hi, g1_hi = g0.astype(BF).astype(F32), g1.astype(BF).astype(F32)
    g0_lo, g1_lo = g0 - g0_hi, g1 - g1_hi

    @pl.loop(0, n_exp * cap // 128)
    def _(i):
        rows = pl.ds(pl.multiple_of(i * 128, 128), 128)
        place = lax.broadcasted_iota(jnp.int32, (128, frames), 0) + i * 128
        at0, at1 = place == tgt0, place == tgt1
        comb_hi[rows, :] = jnp.where(at0, g0_hi, jnp.where(at1, g1_hi, 0.0)).astype(BF)
        comb_lo[rows, :] = jnp.where(at0, g0_lo, jnp.where(at1, g1_lo, 0.0)).astype(BF)

    @pl.loop(1, 2 * NX)
    def _(i):
        wo_copy(i).wait_recv()

    own_o.wait()
    own_f.wait()

    def hidden(r):
        rows = c_rows(r)
        mixed = jnp.concatenate([ctx[b, rows] for b in range(2 * NX)], 1)
        hid[rows, :] = (
            fbuf[rows, :].astype(F32) + jnp.dot(mixed, wo[...], preferred_element_type=F32)
        ).astype(BF)

    hidden(1)
    c2(0)
    c3(0)
    hidden(0)
    pl.semaphore_wait(know.at[2], NY - 1)

    def spot(i):
        return i % 2 * NX + i // 2 % 2 * 2 + i // 4

    def tm_at(p, sign):
        dy, dz = offsets[p]
        return (y + NY + sign * dy) % NY * nz + (z + nz + sign * dz) % nz

    def x_rows(p):
        return pl.ds(p * cap, cap)

    def d_copy(p):
        if p == 0:
            return pltpu.make_async_copy(sbuf.at[p], xbuf.at[spot(m), :, x_rows(p)], d_r.at[p])
        return remote(
            sbuf.at[p], xbuf.at[spot(m), :, x_rows(p)], d_s.at[p], d_r.at[p], tm=tm_at(p, -1)
        )

    def d_wait(p):
        if p == 0:
            d_copy(p).wait()
        else:
            d_copy(p).wait_recv()

    sent_rows = n_tm * 2 * cap // 4
    for i in range(4):
        sent = jnp.dot(
            onehot[i * sent_rows : (i + 1) * sent_rows, :], hid[...], preferred_element_type=F32
        )
        sbuf[i * n_tm // 4 : (i + 1) * n_tm // 4] = sent.astype(BF).reshape(n_tm // 4, 2, cap, 128)
        for p in range(i * n_tm // 4, (i + 1) * n_tm // 4):
            d_copy(p).start()

    def e_rows(j):
        return pl.ds(pl.multiple_of(j // 2 * rc, rc), rc)

    def ex(j, k, ref, dev):
        return remote(ref, ref, e_s.at[j, k], e_r.at[j, k], mp=dev)

    def e_blk(j, blk):
        return xbuf.at[spot(blk), j % 2, e_rows(j)]

    def e_half(j, h, blk):
        rows = pl.ds(pl.multiple_of(j // 2 * rc + h * (rc // 2), rc // 2), rc // 2)
        return xbuf.at[spot(blk), j % 2, rows]

    def e_pair(j, core, odd):
        return xbuf.at[pl.ds(core * NX + odd * 2, 2), j % 2, e_rows(j)]

    near, same = (x + 1) % 2, x % 2

    def e1(j):
        for k in range(parts):

            @pl.when(j == 2 * k)
            def _(k=k):
                for p in range(k * per, (k + 1) * per):
                    d_wait(p)

        ex(j, 0, e_blk(j, m), m_r).start()
        ex(j, 1, e_blk(j, m), m_l).start()

    def e2(j):
        ex(j, 0, e_blk(j, m_l), m_r).wait_recv()
        ex(j, 2, e_half(j, 0, m_l), m_r).start()
        ex(j, 1, e_blk(j, m_r), m_l).wait_recv()
        ex(j, 3, e_half(j, 1, m_r), m_l).start()
        ex(j, 4, e_pair(j, c, near), m_s).start()

    def e3(j):
        ex(j, 2, e_half(j, 0, m_o), m_r).wait_recv()
        ex(j, 3, e_half(j, 1, m_o), m_l).wait_recv()
        ex(j, 5, e_pair(j, c, same), m_s).start()

    def e4(j):
        ex(j, 4, e_pair(j, 1 - c, near), m_s).wait_recv()
        ex(j, 5, e_pair(j, 1 - c, same), m_s).wait_recv()

    def e_sent(j):
        ex(j, 0, e_blk(j, m), m_r).wait_send()
        ex(j, 1, e_blk(j, m), m_l).wait_send()
        ex(j, 2, e_half(j, 0, m_l), m_r).wait_send()
        ex(j, 3, e_half(j, 1, m_r), m_l).wait_send()
        ex(j, 4, e_pair(j, c, near), m_s).wait_send()
        ex(j, 5, e_pair(j, c, same), m_s).wait_send()

    def g_sib(j):
        return remote(psend.at[j], precv.at[j], g_s.at[j, 0], g_r.at[j, 0], mp=m_s)

    def g_far(j, h, dev):
        return remote(q2.at[j, h], r2.at[j, h], g_s.at[j, 1 + h], g_r.at[j, 1 + h], mp=dev)

    def g_near(j, h, dev):
        return remote(q1.at[j, h], r1.at[j, h], g_s.at[j, 3 + h], g_r.at[j, 3 + h], mp=dev)

    def experts(j):
        e4(j)
        e = j % 2
        v = jnp.concatenate([xbuf[spot(b), e, e_rows(j)] for b in range(2 * NX)], 1).astype(F32)
        inv = lax.rsqrt(jnp.mean(v * v, 1, keepdims=True) + EPS)
        normed = (v * inv).astype(BF)
        g = jnp.dot(normed, wg[e], preferred_element_type=F32)
        u = jnp.dot(normed, wu[e], preferred_element_type=F32)
        abuf[...] = (g / (1.0 + jnp.exp(-g)) * u).astype(BF)
        w_far = jnp.concatenate([wd[e, :, col(i * 2 + 1 - c)] for i in range(NX)], 1)
        o_far = jnp.dot(abuf[...], w_far, preferred_element_type=F32).astype(BF)
        for i in range(NX):
            psend[j, i] = o_far[:, i * 128 : (i + 1) * 128]
        g_sib(j).start()
        w_own = jnp.concatenate([wd[e, :, col(i * 2 + c)] for i in range(NX)], 1)
        o_own = jnp.dot(abuf[...], w_own, preferred_element_type=F32)
        for i in range(NX):
            pown[j, i] = o_own[:, i * 128 : (i + 1) * 128]

    halves = (slice(0, rc // 2), slice(rc // 2, rc))

    def both(j, blk, rows=slice(None)):
        return pown[j, blk, rows] + precv[j, blk, rows].astype(F32)

    def g1(j):
        g_sib(j).wait_recv()
        q2[j, 0] = both(j, x_o, halves[0]).astype(BF)
        g_far(j, 0, m_r).start()
        q2[j, 1] = both(j, x_o, halves[1]).astype(BF)
        g_far(j, 1, m_l).start()
        q1[j, 0, halves[1]] = both(j, x_r, halves[1]).astype(BF)
        q1[j, 1, halves[0]] = both(j, x_l, halves[0]).astype(BF)

    def g2(j):
        g_far(j, 0, m_r).wait_recv()
        q1[j, 0, halves[0]] = (both(j, x_r, halves[0]) + r2[j, 0].astype(F32)).astype(BF)
        g_near(j, 0, m_r).start()
        g_far(j, 1, m_l).wait_recv()
        q1[j, 1, halves[1]] = (both(j, x_l, halves[1]) + r2[j, 1].astype(F32)).astype(BF)
        g_near(j, 1, m_l).start()

    def h_copy(p):
        k, i = divmod(p, per)
        src = hsend.at[k, :, pl.ds(i * cap, cap), :]
        if p == 0:
            return pltpu.make_async_copy(src, rbuf.at[p], h_r.at[p])
        return remote(src, rbuf.at[p], h_s.at[p], h_r.at[p], tm=tm_at(p, 1))

    def g3(j):
        g_near(j, 0, m_r).wait_recv()
        g_near(j, 1, m_l).wait_recv()
        hsend[j // 2, j % 2] = (
            both(j, x) + r1[j, 0].astype(F32) + r1[j, 1].astype(F32)
        ).astype(BF)

        for k in range(parts):

            @pl.when(j == 2 * k + 1)
            def _(k=k):
                for p in range(k * per, (k + 1) * per):
                    h_copy(p).start()

    def g_sent(j):
        g_sib(j).wait_send()
        g_far(j, 0, m_r).wait_send()
        g_far(j, 1, m_l).wait_send()
        g_near(j, 0, m_r).wait_send()
        g_near(j, 1, m_l).wait_send()

    own_g.wait()
    own_u.wait()
    own_d.wait()

    def stage(k, f):
        @pl.when((k >= 0) & (k < chunks))
        def _():
            f(k)

    @pl.loop(0, chunks + AHEAD[-1])
    def _(tick):
        for k in ORDER:
            stage(tick - AHEAD[k], (e1, e2, e3, experts, g1, g2, g3)[k])

    def sent():
        halo_k.wait_send()
        halo_v.wait_send()

        @pl.loop(1, 2 * NX)
        def _(i):
            wo_copy(i).wait_send()

        @pl.loop(0, 2)
        def _(r):
            c_sent(r)

        @pl.loop(0, chunks)
        def _(j):
            e_sent(j)
            g_sent(j)

        for p in range(1, n_tm):
            d_copy(p).wait_send()
        for p in range(1, (parts - 1) * per):
            h_copy(p).wait_send()

    acc[...] = jnp.zeros_like(acc)
    for k in range(parts):
        if k == parts - 1:
            sent()
        mine = range(k * per, (k + 1) * per)
        for p in mine:
            if p == 0:
                h_copy(p).wait()
            else:
                h_copy(p).wait_recv()
        rows = slice(2 * rc * k, 2 * rc * (k + 1))
        back = rbuf[mine.start : mine.stop].reshape(2 * rc, 128)
        back_t = back.astype(F32).T.astype(BF)
        acc[...] += jnp.dot(back_t, comb_hi[rows, :], preferred_element_type=F32) + jnp.dot(
            back_t, comb_lo[rows, :], preferred_element_type=F32
        )

    out_ref[...] = (hid[...].astype(F32) + acc[...].T).astype(BF)

    for p in range((parts - 1) * per, n_tm):
        if p > 0:
            h_copy(p).wait_send()


def per_device(
    frames_in,
    queries,
    keys,
    values,
    segment_edges,
    out_proj,
    expert_ids,
    gates,
    w_gate,
    w_up,
    w_down,
):
    frames = frames_in.shape[0]
    n_tm = lax.axis_size("tm")
    model = frames_in.shape[1]
    inner = w_gate.shape[2]
    n_exp = w_gate.shape[0] * n_tm
    cap = 4 * frames // n_exp
    parts = PARTS
    chunks = 2 * parts
    rc = n_tm // parts * cap
    slots = n_exp * cap
    vmem = pl.BlockSpec(memory_space=pltpu.VMEM)
    anyw = pl.BlockSpec(memory_space=pl.ANY)
    dma = pltpu.SemaphoreType.DMA
    return pl.pallas_call(
        functools.partial(kernel, n_tm, cap, parts),
        out_shape=jax.ShapeDtypeStruct((frames, 128), BF),
        in_specs=[vmem] * 4 + [anyw] * 7,
        out_specs=vmem,
        scratch_shapes=[
            pltpu.VMEM((LEFT + frames, 128), BF),
            pltpu.VMEM((LEFT + frames, 128), BF),
            pltpu.VMEM((frames, 128), BF),
            pltpu.VMEM((model, 128), BF),
            pltpu.VMEM(w_gate.shape, BF),
            pltpu.VMEM(w_up.shape, BF),
            pltpu.VMEM(w_down.shape, BF),
            pltpu.VMEM((model // 128, frames, 128), BF),
            pltpu.VMEM((frames, 128), BF),
            pltpu.VMEM((slots, frames), BF),
            pltpu.VMEM((slots, frames), BF),
            pltpu.VMEM((slots, frames), BF),
            pltpu.VMEM((n_tm, 2, cap, 128), BF),
            pltpu.VMEM((model // 128, 2, n_tm * cap, 128), BF),
            pltpu.VMEM((rc, inner), BF),
            pltpu.VMEM((chunks, NX, rc, 128), F32),
            pltpu.VMEM((chunks, NX, rc, 128), BF),
            pltpu.VMEM((chunks, NX, rc, 128), BF),
            pltpu.VMEM((chunks, 2, rc // 2, 128), BF),
            pltpu.VMEM((chunks, 2, rc // 2, 128), BF),
            pltpu.VMEM((chunks, 2, rc, 128), BF),
            pltpu.VMEM((chunks, 2, rc, 128), BF),
            pltpu.VMEM((parts, 2, rc, 128), BF),
            pltpu.VMEM((n_tm, 2, cap, 128), BF),
            pltpu.VMEM((128, frames), F32),
            dma((7,)),
            dma((2,)),
            dma((2,)),
            dma((2 * NX,)),
            dma((2 * NX,)),
            dma((2, 8)),
            dma((2, 8)),
            dma((n_tm,)),
            dma((n_tm,)),
            dma((chunks, 6)),
            dma((chunks, 6)),
            dma((chunks, 5)),
            dma((chunks, 5)),
            dma((n_tm,)),
            dma((n_tm,)),
            pltpu.SemaphoreType.REGULAR((3,)),
        ],
        compiler_params=pltpu.CompilerParams(
            collective_id=0, has_side_effects=True, vmem_limit_bytes=56 * 1024 * 1024
        ),
        name="layer",
    )(
        segment_edges,
        expert_ids.T,
        gates.T,
        queries,
        keys,
        values,
        frames_in,
        out_proj,
        w_gate,
        w_up,
        w_down,
    )


def solution(mesh):
    return jax.shard_map(
        per_device,
        mesh=mesh,
        in_specs=(
            P("tm", None),
            P("tm", "mp"),
            P("tm", "mp"),
            P("tm", "mp"),
            P(None, "tm"),
            P("mp", None),
            P("tm", None),
            P("tm", None),
            P("tm", None, "mp"),
            P("tm", None, "mp"),
            P("tm", "mp", None),
        ),
        out_specs=P("tm", "mp"),
        check_vma=False,
    )
```
